32 devices in a mesh: tm: 8 (over z, y), stream: 4 (over x, core).
Axes of the slice: x: 2, y: 2, z: 4, core: 2. Of those that a mesh axis runs over, the one named last changes fastest.
Arguments:
- signal: bfloat16 [4, 49152, 256], P('stream', 'tm'), may hold values from -6 to 6
- lengths: int32 [4], P('stream'), may hold values from 12288 to 49152, as said below
- w_conv: bfloat16 [512, 512], replicated, may hold values from -0.25 to 0.25
- w_res: bfloat16 [256, 256], replicated, may hold values from -0.375 to 0.375
- w_in: bfloat16 [256, 1024], replicated, may hold values from -0.375 to 0.375
- w_qkv: bfloat16 [1024, 3072], P(None, 'stream')
- w_out: bfloat16 [1024, 1024], P('stream'), may hold values from -0.1875 to 0.1875
- d_out: bfloat16 [4, 192, 1024], P('stream', 'tm'), may hold values from -6 to 6
Outputs:
- out: bfloat16 [4, 192, 1024], P('stream', 'tm')
- d_signal: bfloat16 [4, 49152, 256], P('stream', 'tm')
- g_conv: float32 [512, 512], P('stream')
- g_res: float32 [256, 256], P('stream')
- g_in: float32 [256, 1024], P('stream')
- g_qkv: float32 [1024, 3072], P('tm', 'stream')
- g_out: float32 [1024, 1024], P('stream', 'tm')
The draws below stay inside these ranges and needn't reach their ends.
Inputs may be any that keep to these rules, and one draw needn't show every extreme that they name: `lengths`: some stay has all 49152 samples valid and some other stay exactly 12288.
All inputs are finite; a program needn't handle non-finite values.
Results may differ from the reference program's by a relative error of at most 0.013.
Values may be sent and summed in bfloat16 or wider, within the bound.
A program may use at most 128 MiB of HBM per device.

```python
import math
import jax
import jax.numpy as jnp
from jax import lax

CONV_CHANNELS = 256
D = 1024
HEADS = 16
HEAD = 64
POOL = 256
DILATION_STEP = 512
STAYS = 4
STAY_SAMPLES = 49152
TOKENS = 192


def draw_lengths(key, part):
    values = jax.random.randint(key, (STAYS,), STAY_SAMPLES // 4, STAY_SAMPLES + 1)
    where_full = jax.random.randint(jax.random.fold_in(key, 11), (), 0, STAYS)
    where_short = (where_full + 1) % STAYS
    places = jnp.arange(STAYS)
    values = jnp.where(places == where_full, STAY_SAMPLES, values)
    values = jnp.where(places == where_short, STAY_SAMPLES // 4, values)
    return values.astype(jnp.int32)


def draw_w_qkv(key, part):
    base = jax.random.normal(key, (D, HEADS, 3, D // HEADS), jnp.float32) / math.sqrt(D)
    return base.reshape(D, 3 * D).astype(jnp.bfloat16)


def block_scale(own_key, extent, pieces, low, high):
    loudness, own = 1.0, jax.random.fold_in(own_key, 6)
    for dim, shards_of in pieces:
        draws = jnp.exp(jax.random.uniform(jax.random.fold_in(own, dim), (shards_of,), jnp.float32, low / len(pieces), high / len(pieces)))
        loudness = loudness * jnp.repeat(draws, extent[dim] // shards_of).reshape([-1 if axis == dim else 1 for axis in range(len(extent))])
    return loudness


def scatter_about(own_key, shape, spread, bound, split=(), held_as=jnp.bfloat16):
    level = block_scale(own_key, shape, split, -0.22, 0.18) if split else 1.0
    values = jax.random.normal(own_key, shape, jnp.float32) * spread * level
    return jnp.minimum(jnp.maximum(values, -bound), bound).astype(held_as)


def setup_inputs(seed: int = 0) -> dict:
    key_of = jax.random.split(jax.random.key(seed), 9)
    return {
        "signal": scatter_about(key_of[0], (STAYS, STAY_SAMPLES, CONV_CHANNELS), 1.0, 6.0, ((0, 4), (1, 8))),
        "lengths": draw_lengths(jax.random.fold_in(key_of[8], 71), 0),
        "w_conv": scatter_about(key_of[2], (2 * CONV_CHANNELS, 2 * CONV_CHANNELS), (2 * CONV_CHANNELS) ** -0.5, 0.25),
        "w_res": scatter_about(key_of[3], (CONV_CHANNELS, CONV_CHANNELS), CONV_CHANNELS ** -0.5, 0.375),
        "w_in": scatter_about(key_of[4], (CONV_CHANNELS, D), CONV_CHANNELS ** -0.5, 0.375),
        "w_qkv": draw_w_qkv(jax.random.fold_in(key_of[8], 71), 0),
        "w_out": scatter_about(key_of[6], (D, D), D ** -0.5, 0.1875, ((0, 4),)),
        "d_out": scatter_about(key_of[7], (STAYS, TOKENS, D), 1.0, 6.0, ((0, 4), (1, 8))),
    }


EPS = 1e-05
HIGH = lax.Precision.HIGHEST

def conv_parts(stay_signal_rows, length, w_conv):
    past_rows = jnp.concatenate([jnp.zeros((DILATION_STEP, CONV_CHANNELS), stay_signal_rows.dtype), stay_signal_rows[:STAY_SAMPLES - DILATION_STEP]], axis=0)
    joined = jnp.concatenate([past_rows, stay_signal_rows], axis=1)
    mixed = jnp.dot(joined, w_conv, preferred_element_type=jnp.float32)
    tanh_f = jnp.tanh(mixed[:, :CONV_CHANNELS])
    sig_g = jax.nn.sigmoid(mixed[:, CONV_CHANNELS:])
    hidden = (tanh_f * sig_g).astype(jnp.bfloat16)
    valid = (jnp.arange(STAY_SAMPLES) < length)[:, None]
    return (joined, tanh_f, sig_g, hidden, valid)

def reference(signal, lengths, w_conv, w_res, w_in, w_qkv, w_out, d_out):

    def stay_forward(pair):
        stay_signal_rows, length = pair
        joined, tanh_f, sig_g, hidden, valid = conv_parts(stay_signal_rows, length, w_conv)
        resid = jnp.where(valid, stay_signal_rows.astype(jnp.float32) + jnp.dot(hidden, w_res, preferred_element_type=jnp.float32), 0.0)
        return lax.optimization_barrier(jnp.mean(resid.reshape(TOKENS, POOL, CONV_CHANNELS), axis=1)).astype(jnp.bfloat16)
    pooled = lax.map(stay_forward, (signal, lengths))
    pooled_flat = pooled.reshape(STAYS * TOKENS, CONV_CHANNELS)
    tokens = jnp.dot(pooled_flat, w_in, preferred_element_type=jnp.float32).astype(jnp.bfloat16)
    tok_values = tokens.astype(jnp.float32)
    tok_scale = lax.rsqrt(lax.optimization_barrier(jnp.mean(tok_values * tok_values, axis=-1, keepdims=True)) + EPS)
    normed = (tok_values * tok_scale).astype(jnp.bfloat16)
    proj = jnp.dot(normed, w_qkv, preferred_element_type=jnp.float32).astype(jnp.bfloat16)
    proj = proj.reshape(STAYS, TOKENS, HEADS, 3, HEAD).astype(jnp.float32)
    query = proj[:, :, :, 0]
    keys = proj[:, :, :, 1]
    values = proj[:, :, :, 2]
    scale = 1.0 / math.sqrt(HEAD)
    position = jnp.arange(TOKENS)
    allowed = (position[None, None, :] <= position[None, :, None]) & ((position * POOL)[None, None, :] < lengths[:, None, None])
    scores = jnp.einsum('sqhe,skhe->shqk', query, keys, precision=HIGH) * scale
    scores = jnp.where(allowed[:, None], scores, -1e+30)
    top = lax.optimization_barrier(jnp.max(scores, axis=-1, keepdims=True))
    weights = jnp.exp(scores - top)
    prob = weights / lax.optimization_barrier(jnp.sum(weights, axis=-1, keepdims=True))
    prob16 = prob.astype(jnp.bfloat16).astype(jnp.float32)
    context = jnp.einsum('shqk,skhe->sqhe', prob16, values, precision=HIGH).astype(jnp.bfloat16)
    context = context.reshape(STAYS * TOKENS, D)
    part = jnp.dot(context, w_out, preferred_element_type=jnp.float32)
    out = (tok_values + part).astype(jnp.bfloat16).reshape(STAYS, TOKENS, D)
    grad_flat = d_out.reshape(STAYS * TOKENS, D)
    g_out = jnp.dot(context.T, grad_flat, preferred_element_type=jnp.float32)
    d_context = jnp.dot(grad_flat, w_out.T, preferred_element_type=jnp.float32).astype(jnp.bfloat16)
    d_context = d_context.reshape(STAYS, TOKENS, HEADS, HEAD).astype(jnp.float32)
    d_prob = jnp.einsum('sqhe,skhe->shqk', d_context, values, precision=HIGH)
    d_score = prob * (d_prob - lax.optimization_barrier(jnp.sum(d_prob * prob, axis=-1, keepdims=True)))
    d_query = scale * jnp.einsum('shqk,skhe->sqhe', d_score, keys, precision=HIGH)
    d_keys = scale * jnp.einsum('shqk,sqhe->skhe', d_score, query, precision=HIGH)
    d_values = jnp.einsum('shqk,sqhe->skhe', prob16, d_context, precision=HIGH)
    d_proj = jnp.stack([d_query, d_keys, d_values], axis=3).reshape(STAYS * TOKENS, 3 * D)
    g_qkv = jnp.dot(normed.astype(jnp.float32).T, d_proj, precision=HIGH)
    d_normed = jnp.dot(d_proj, w_qkv.astype(jnp.float32).T, precision=HIGH)
    inner = lax.optimization_barrier(jnp.sum(d_normed * tok_values, axis=-1, keepdims=True))
    cube = tok_scale * tok_scale * tok_scale
    d_tokens = grad_flat.astype(jnp.float32) + tok_scale * d_normed - tok_values * cube * inner / D
    g_in = jnp.dot(pooled_flat.astype(jnp.float32).T, d_tokens, precision=HIGH)
    d_pooled = jnp.dot(d_tokens, w_in.astype(jnp.float32).T, precision=HIGH).reshape(STAYS, TOKENS, CONV_CHANNELS)

    def stay_backward(triple):
        stay_signal_rows, length, d_pool = triple
        joined, tanh_f, sig_g, hidden, valid = conv_parts(stay_signal_rows, length, w_conv)
        d_resid = jnp.where(valid, jnp.repeat(d_pool / POOL, POOL, axis=0), 0.0).astype(jnp.bfloat16)
        res_grad = jnp.dot(hidden.T, d_resid, preferred_element_type=jnp.float32)
        d_hidden = jnp.dot(d_resid, w_res.T, preferred_element_type=jnp.float32)
        d_mixed = jnp.concatenate([d_hidden * (1.0 - tanh_f * tanh_f) * sig_g, d_hidden * tanh_f * sig_g * (1.0 - sig_g)], axis=1).astype(jnp.bfloat16)
        conv_grad = jnp.dot(joined.T, d_mixed, preferred_element_type=jnp.float32)
        d_joined = jnp.dot(d_mixed, w_conv.T, preferred_element_type=jnp.float32)
        past_gradient = d_joined[:, :CONV_CHANNELS].astype(jnp.bfloat16)
        later_gradient = jnp.concatenate([past_gradient[DILATION_STEP:], jnp.zeros((DILATION_STEP, CONV_CHANNELS), past_gradient.dtype)], axis=0)
        d_stay = (d_resid.astype(jnp.float32) + d_joined[:, CONV_CHANNELS:] + later_gradient.astype(jnp.float32)).astype(jnp.bfloat16)
        return (d_stay, conv_grad, res_grad)
    d_signal, conv_grads, res_grads = lax.map(stay_backward, (signal, lengths, d_pooled))
    return (out, d_signal, lax.optimization_barrier(jnp.sum(conv_grads, axis=0)), lax.optimization_barrier(jnp.sum(res_grads, axis=0)), g_in, g_qkv, g_out)
```

```python
import functools
import math

import jax
import jax.numpy as jnp
from jax import lax
from jax.experimental import pallas as pl
from jax.experimental.pallas import tpu as pltpu
from jax.sharding import PartitionSpec as P

HEADS = 16
POOL = 256
DILATION_STEP = 512
EPS = 1e-05
BF16 = jnp.bfloat16
F32 = jnp.float32
HIGH = lax.Precision.HIGHEST
MESH = pl.DeviceIdType.MESH
VMEM_SPEC = pl.BlockSpec(memory_space=pltpu.VMEM)


def dot(eq, a, b):
    return jnp.einsum(eq, a, b, preferred_element_type=F32)


def exchange_kernel(axis, n, kinds, *refs):
    k = len(kinds)
    ins, outs = refs[:k], refs[k : 2 * k]
    rest = list(refs[2 * k :])
    slots = [rest.pop(0) if kind.startswith("reduce") or kind == "gatherf" else None for kind in kinds]
    send, recv, local_sem = rest
    me = lax.axis_index(axis)
    barrier = pltpu.get_barrier_semaphore()
    for d in range(1, n):
        pl.semaphore_signal(
            barrier, inc=1, device_id={axis: lax.rem(me + d, n)}, device_id_type=MESH
        )
    pl.semaphore_wait(barrier, n - 1)
    copies = []
    locals_ = []
    for j, kind in enumerate(kinds):
        for d in range(1, n):
            peer = lax.rem(me + d, n)
            src = ins[j] if kind.startswith("gather") else ins[j].at[peer]
            if kind.startswith("reduce"):
                dst = slots[j].at[d - 1]
            elif kind == "gatherf":
                dst = slots[j].at[me]
            elif kind.endswith("1"):
                dst = outs[j].at[:, me]
            else:
                dst = outs[j].at[me]
            copy = pltpu.make_async_remote_copy(
                src_ref=src,
                dst_ref=dst,
                send_sem=send.at[j, d - 1],
                recv_sem=recv.at[j, d - 1],
                device_id={axis: peer},
                device_id_type=MESH,
            )
            copy.start()
            copies.append(copy)
        if not kind.startswith("reduce"):
            src = ins[j] if kind.startswith("gather") else ins[j].at[me]
            land = slots[j] if kind == "gatherf" else outs[j]
            dst = land.at[:, me] if kind.endswith("1") else land.at[me]
            copy = pltpu.make_async_copy(src, dst, local_sem.at[j])
            copy.start()
            locals_.append(copy)
    for copy in locals_:
        copy.wait()
    for copy in copies:
        copy.wait()
    for j, kind in enumerate(kinds):
        if kind.startswith("reduce"):
            total = ins[j][me].astype(F32)
            for d in range(1, n):
                total += slots[j][d - 1].astype(F32)
            outs[j][...] = total.astype(outs[j].dtype)
        elif kind == "gatherf":
            outs[j][...] = slots[j][...].astype(F32)


def exchange(axis, collective, items):
    n = lax.axis_size(axis)
    kinds = tuple(kind for kind, _ in items)
    arrays = [array for _, array in items]
    shapes, slots = [], []
    for kind, array in items:
        inner = array.shape if kind.startswith("gather") else array.shape[1:]
        if kind.startswith("reduce"):
            shapes.append(jax.ShapeDtypeStruct(inner, BF16 if kind == "reduceb" else F32))
            slots.append(pltpu.VMEM((n - 1,) + inner, array.dtype))
        elif kind == "gatherf":
            shapes.append(jax.ShapeDtypeStruct((n,) + inner, F32))
            slots.append(pltpu.VMEM((n,) + inner, array.dtype))
        elif kind.endswith("1"):
            shapes.append(jax.ShapeDtypeStruct((inner[0], n) + inner[1:], array.dtype))
        else:
            shapes.append(jax.ShapeDtypeStruct((n,) + inner, array.dtype))
    k = len(items)
    return pl.pallas_call(
        functools.partial(exchange_kernel, axis, n, kinds),
        out_shape=shapes,
        in_specs=[VMEM_SPEC] * k,
        out_specs=[VMEM_SPEC] * k,
        scratch_shapes=slots
        + [
            pltpu.SemaphoreType.DMA((k, n - 1)),
            pltpu.SemaphoreType.DMA((k, n - 1)),
            pltpu.SemaphoreType.DMA((k,)),
        ],
        compiler_params=pltpu.CompilerParams(collective_id=collective, has_side_effects=True),
        name=f"exchange_{axis}_{collective}",
    )(*arrays)


def attention_kernel(heads, size, scale, len_ref, proj_ref, dctx_ref, ctx_ref, dproj_ref):
    stay = pl.program_id(0)
    total = proj_ref.shape[1]
    length = len_ref[stay]
    row = lax.broadcasted_iota(jnp.int32, (total, total), 0)
    col = lax.broadcasted_iota(jnp.int32, (total, total), 1)
    allowed = (col <= row) & (col * POOL < length)
    nt = (((1,), (1,)), ((), ()))
    tn = (((0,), (0,)), ((), ()))
    for h in range(heads):
        base = h * 3 * size
        query = proj_ref[0, :, base : base + size]
        key = proj_ref[0, :, base + size : base + 2 * size]
        value = proj_ref[0, :, base + 2 * size : base + 3 * size]
        dctx = dctx_ref[0, :, h * size : (h + 1) * size]
        scores = lax.dot_general(query, key, nt, preferred_element_type=F32) * scale
        scores = jnp.where(allowed, scores, -1e30)
        top = jnp.max(scores, axis=-1, keepdims=True)
        weights = jnp.exp(scores - top)
        prob = weights / jnp.sum(weights, axis=-1, keepdims=True)
        prob16 = prob.astype(BF16)
        context = jnp.dot(prob16, value, preferred_element_type=F32)
        ctx_ref[0, :, h * size : (h + 1) * size] = context.astype(BF16)
        d_prob = lax.dot_general(dctx, value, nt, preferred_element_type=F32)
        d_score = prob * (d_prob - jnp.sum(d_prob * prob, axis=-1, keepdims=True))
        d16 = d_score.astype(BF16)
        d_query = scale * jnp.dot(d16, key, preferred_element_type=F32)
        d_key = scale * lax.dot_general(d16, query, tn, preferred_element_type=F32)
        d_value = lax.dot_general(prob16, dctx, tn, preferred_element_type=F32)
        dproj_ref[0, :, base : base + size] = d_query.astype(BF16)
        dproj_ref[0, :, base + size : base + 2 * size] = d_key.astype(BF16)
        dproj_ref[0, :, base + 2 * size : base + 3 * size] = d_value.astype(BF16)


def attention(proj, d_context, group_len, heads, size):
    group, total, width = proj.shape
    inner = heads * size
    wide = pl.BlockSpec((1, total, width), lambda s: (s, 0, 0))
    thin = pl.BlockSpec((1, total, inner), lambda s: (s, 0, 0))
    return pl.pallas_call(
        functools.partial(attention_kernel, heads, size, 1.0 / math.sqrt(size)),
        grid=(group,),
        out_shape=(
            jax.ShapeDtypeStruct((group, total, inner), BF16),
            jax.ShapeDtypeStruct((group, total, width), BF16),
        ),
        in_specs=[pl.BlockSpec(memory_space=pltpu.SMEM), wide, thin],
        out_specs=(thin, wide),
        name="attention",
    )(group_len, proj, d_context)


def riding_copies(axis, kinds, ins, slots, send, recv, keep):
    n = lax.axis_size(axis)
    me = lax.axis_index(axis)
    copies = []
    for j, kind in enumerate(kinds):
        for d in range(1, n):
            peer = lax.rem(me + d, n)
            copies.append(
                pltpu.make_async_remote_copy(
                    src_ref=ins[j] if kind == "gather1" else ins[j].at[peer],
                    dst_ref=slots[j].at[d - 1] if kind == "reduce" else slots[j].at[:, me],
                    send_sem=send.at[j, d - 1],
                    recv_sem=recv.at[j, d - 1],
                    device_id={axis: peer},
                    device_id_type=MESH,
                )
            )
        if kind != "reduce":
            src = ins[j] if kind == "gather1" else ins[j].at[me]
            copies.append(pltpu.make_async_copy(src, slots[j].at[:, me], keep.at[j]))
    return copies


def ride_start(axis, kinds, ins, slots, send, recv, keep):
    n = lax.axis_size(axis)
    me = lax.axis_index(axis)
    barrier = pltpu.get_barrier_semaphore()
    for d in range(1, n):
        pl.semaphore_signal(
            barrier, inc=1, device_id={axis: lax.rem(me + d, n)}, device_id_type=MESH
        )
    pl.semaphore_wait(barrier, n - 1)
    for copy in riding_copies(axis, kinds, ins, slots, send, recv, keep):
        copy.start()


def ride_finish(axis, kinds, ins, outs, slots, send, recv, keep):
    n = lax.axis_size(axis)
    me = lax.axis_index(axis)
    for copy in riding_copies(axis, kinds, ins, slots, send, recv, keep):
        copy.wait()
    for j, kind in enumerate(kinds):
        if kind == "reduce":
            sum_ = ins[j][me].astype(F32)
            for d in range(1, n):
                sum_ += slots[j][d - 1].astype(F32)
            outs[j][...] = sum_
        else:
            outs[j][...] = slots[j][...]


def ride_shapes(n, items):
    shapes, scratch = [], []
    for kind, array in items:
        inner = array.shape if kind == "gather1" else array.shape[1:]
        if kind == "reduce":
            shapes.append(jax.ShapeDtypeStruct(inner, F32))
            scratch.append(pltpu.VMEM((n - 1,) + inner, array.dtype))
        else:
            out = (inner[0], n) + inner[1:]
            shapes.append(jax.ShapeDtypeStruct(out, array.dtype))
            scratch.append(pltpu.VMEM(out, array.dtype))
    k = len(items)
    sems = [pltpu.SemaphoreType.DMA((k, n - 1))] * 2 + [pltpu.SemaphoreType.DMA((k,))]
    specs = [pl.BlockSpec(a.shape, functools.partial(origin, a.ndim)) for _, a in items]
    outs = [pl.BlockSpec(a.shape, functools.partial(origin, len(a.shape))) for a in shapes]
    return shapes, scratch + sems, specs, outs


def origin(rank, i):
    return (0,) * rank


def tile_valid(info_ref, tile, step):
    row = lax.broadcasted_iota(jnp.int32, (tile, 1), 0)
    return info_ref[0] + step * tile + row < info_ref[1]


def joined_tile(first, in_ref, past_ref, cur_ref):
    past = jnp.where(first, in_ref[...], past_ref[...])
    return jnp.concatenate([past, cur_ref[...]], axis=1)


def backward_kernel(
    steps, axis, kinds, info_ref, in_ref, past_ref, cur_ref, a_ref, dh_ref, dr_ref, w_ref,
    *refs,
):
    k = len(kinds)
    ins, (sig_ref, first_ref, g_ref) = refs[:k], refs[k : k + 3]
    outs, (acc_ref, later_ref) = refs[k + 3 : 2 * k + 3], refs[2 * k + 3 : 2 * k + 5]
    slots, sems = refs[2 * k + 5 : 3 * k + 5], refs[3 * k + 5 :]
    i = pl.program_id(0)

    @pl.when(i == 0)
    def _():
        ride_start(axis, kinds, ins, slots, *sems)

    step = steps - 1 - i
    tile, chans = cur_ref.shape

    @pl.when(i == 0)
    def _():
        acc_ref[...] = jnp.zeros_like(acc_ref)
        later_ref[...] = jnp.zeros_like(later_ref)

    joined = joined_tile(step == 0, in_ref, past_ref, cur_ref)
    valid = tile_valid(info_ref, tile, step)

    def spread(ref):
        pieces = [
            jnp.broadcast_to(ref[0, j : j + 1, :], (POOL, chans)) for j in range(tile // POOL)
        ]
        return jnp.where(valid, jnp.concatenate(pieces, axis=0), 0.0)

    d_hidden = spread(dh_ref)
    d_mixed = (
        a_ref[...].astype(F32) * jnp.concatenate([d_hidden, d_hidden], axis=1)
    ).astype(BF16)
    acc_ref[...] += lax.dot_general(
        joined, d_mixed, (((0,), (0,)), ((), ())), preferred_element_type=F32
    )
    d_joined = lax.dot_general(
        d_mixed, w_ref[...], (((1,), (1,)), ((), ())), preferred_element_type=F32
    )
    sig_ref[...] = (spread(dr_ref) + d_joined[:, chans:] + later_ref[...].astype(F32)).astype(BF16)
    later_ref[...] = d_joined[:, :chans].astype(BF16)

    @pl.when(i == steps - 1)
    def _():
        first_ref[...] = d_joined[:, :chans].astype(BF16)
        g_ref[...] = acc_ref[...].astype(BF16)
        ride_finish(axis, kinds, ins, outs, slots, *sems)


def final_kernel(axis, n, *refs):
    ins, outs, slots, mine, lands = refs[:3], refs[3:6], refs[6:8], refs[8:10], refs[10:13]
    send, recv, keep = refs[13:]
    me = lax.axis_index(axis)
    barrier = pltpu.get_barrier_semaphore()
    for d in range(1, n):
        pl.semaphore_signal(
            barrier, inc=1, device_id={axis: lax.rem(me + d, n)}, device_id_type=MESH
        )
    pl.semaphore_wait(barrier, n - 1)

    def push(row, d, src, dst):
        copy = pltpu.make_async_remote_copy(
            src_ref=src,
            dst_ref=dst,
            send_sem=send.at[row, d - 1],
            recv_sem=recv.at[row, d - 1],
            device_id={axis: lax.rem(me + d, n)},
            device_id_type=MESH,
        )
        copy.start()
        return copy

    parts = [
        push(j, d, ins[j].at[lax.rem(me + d, n)], slots[j].at[d - 1])
        for j in range(2)
        for d in range(1, n)
    ]
    rest = [push(2, d, ins[2], lands[2].at[me]) for d in range(1, n)]
    for copy in parts:
        copy.wait()
    for j in range(2):
        total = ins[j][me].astype(F32)
        for d in range(1, n):
            total += slots[j][d - 1].astype(F32)
        mine[j][...] = total.astype(BF16)
    for j, src in enumerate((mine[0], mine[1], ins[2])):
        copy = pltpu.make_async_copy(src, lands[j].at[me], keep.at[j])
        copy.start()
        rest.append(copy)
    rest += [push(3 + j, d, mine[j], lands[j].at[me]) for j in range(2) for d in range(1, n)]
    for copy in rest:
        copy.wait()
    for j in range(3):
        outs[j][...] = lands[j][...].astype(F32)


def final_sums(axis, collective, conv, res, cols):
    n = lax.axis_size(axis)
    shapes = [conv.shape, res.shape, (n,) + cols.shape]
    sums = [conv.shape[1:], res.shape[1:]]
    return pl.pallas_call(
        functools.partial(final_kernel, axis, n),
        out_shape=[jax.ShapeDtypeStruct(a, F32) for a in shapes],
        in_specs=[VMEM_SPEC] * 3,
        out_specs=[VMEM_SPEC] * 3,
        scratch_shapes=[pltpu.VMEM((n - 1,) + a, BF16) for a in sums]
        + [pltpu.VMEM(a, BF16) for a in sums]
        + [pltpu.VMEM(a, BF16) for a in shapes]
        + [pltpu.SemaphoreType.DMA((5, n - 1))] * 2
        + [pltpu.SemaphoreType.DMA((3,))],
        compiler_params=pltpu.CompilerParams(collective_id=collective, has_side_effects=True),
        name="final_sums",
    )(conv, res, cols)


def conv_backward(
    info, incoming, signal, gates, d_hidden, d_resid, w_conv, axis, collective, items
):
    kinds = tuple(kind for kind, _ in items)
    shapes, scratch, specs, out_specs = ride_shapes(lax.axis_size(axis), items)
    samples, chans = signal.shape
    tile = DILATION_STEP
    steps, pools = samples // tile, tile // POOL
    block = pl.BlockSpec((tile, chans), lambda i: (steps - 1 - i, 0))
    fixed = pl.BlockSpec((tile, chans), lambda i: (0, 0))
    sums = pl.BlockSpec((1, pools, chans), lambda i: (steps - 1 - i, 0, 0))
    whole = pl.BlockSpec(w_conv.shape, lambda i: (0, 0))
    return pl.pallas_call(
        functools.partial(backward_kernel, steps, axis, kinds),
        grid=(steps,),
        out_shape=[
            jax.ShapeDtypeStruct((samples, chans), BF16),
            jax.ShapeDtypeStruct((tile, chans), BF16),
            jax.ShapeDtypeStruct(w_conv.shape, BF16),
        ]
        + shapes,
        in_specs=[
            pl.BlockSpec(memory_space=pltpu.SMEM),
            fixed,
            pl.BlockSpec((tile, chans), lambda i: (jnp.maximum(steps - 2 - i, 0), 0)),
            block,
            pl.BlockSpec((tile, 2 * chans), lambda i: (steps - 1 - i, 0)),
            sums,
            sums,
            whole,
        ]
        + specs,
        out_specs=[block, fixed, whole] + out_specs,
        scratch_shapes=[pltpu.VMEM(w_conv.shape, F32), pltpu.VMEM((tile, chans), BF16)] + scratch,
        compiler_params=pltpu.CompilerParams(collective_id=collective, has_side_effects=True),
        name="conv_backward",
    )(info, incoming, signal, signal, gates, d_hidden, d_resid, w_conv, *[a for _, a in items])


def device_of(tm, stream):
    return {"tm": tm, "stream": stream}


def front_kernel(
    steps, group, len_ref, sig_hbm, w_ref, wout_ref, wres_ref, wgrad_ref,
    a_hbm, edge_hbm, hsum_ref, pool_ref, ctx_ref, cols_ref, lens_ref,
    sig, a_buf, grads, gate_w, ctx_mine, cols_mine, sums, sem_in, sem_out, send_tm, recv_tm,
    send_st, recv_st, send_pool, recv_pool, send_near, recv_near, keep,
):
    tms, parts = lax.axis_size("tm"), lax.axis_size("stream")
    tm, st = lax.axis_index("tm"), lax.axis_index("stream")
    chips = parts // 2
    core, chip = lax.rem(st, 2), st // 2
    mine = tm * chips + chip
    tile = DILATION_STEP
    samples = steps * tile
    chans = w_ref.shape[1] // 2
    toks = samples // POOL
    rounds = steps // group

    def peer_of(flat):
        return device_of(flat // chips, lax.rem(flat, chips) * 2 + core)

    barrier = pltpu.get_barrier_semaphore()

    def greet(device):
        pl.semaphore_signal(barrier, inc=1, device_id=device, device_id_type=MESH)

    others = tms * chips
    lax.fori_loop(1, others, lambda d, c: (greet(peer_of(lax.rem(mine + d, others))), c)[1], 0)
    for d in range(chips):
        greet(device_of(tm, lax.rem(chip + d, chips) * 2 + 1 - core))

    def load(i):
        return pltpu.make_async_copy(
            sig_hbm.at[pl.ds(i * tile, tile)], sig.at[pl.ds((i + 1) * tile, tile)], sem_in.at[i]
        )

    def save(i):
        return pltpu.make_async_copy(
            a_buf.at[pl.ds(i * tile, tile)], a_hbm.at[pl.ds(i * tile, tile)], sem_out.at[i]
        )

    for i in reversed(range(steps)):
        load(i).start()
    gate_w[...] = w_ref[:, chans:] * jnp.asarray(0.5, BF16)

    halo = pltpu.make_async_remote_copy(
        src_ref=sig_hbm.at[pl.ds(samples - tile, tile)],
        dst_ref=sig.at[pl.ds(0, tile)],
        send_sem=send_tm.at[2, 0],
        recv_sem=recv_tm.at[2, 0],
        device_id={"tm": lax.rem(tm + 1, tms)},
        device_id_type=MESH,
    )

    def to_stream(j, d, src, dst):
        return pltpu.make_async_remote_copy(
            src_ref=src,
            dst_ref=dst,
            send_sem=send_st.at[j, d - 1],
            recv_sem=recv_st.at[j, d - 1],
            device_id={"stream": lax.rem(st + d, parts)},
            device_id_type=MESH,
        )

    grad_copies = [
        copy
        for d in range(1, parts)
        for copy in (
            to_stream(0, d, wgrad_ref, grads.at[st]),
            to_stream(1, d, lens_ref.at[st], lens_ref.at[st]),
        )
    ]

    def to_tm(j, d, src, dst):
        return pltpu.make_async_remote_copy(
            src_ref=src,
            dst_ref=dst,
            send_sem=send_tm.at[j, d - 1],
            recv_sem=recv_tm.at[j, d - 1],
            device_id={"tm": lax.rem(tm + d, tms)},
            device_id_type=MESH,
        )

    width = grads.shape[2]
    columns = width // tms

    tm_copies = [
        copy
        for d in range(1, tms)
        for copy in (
            to_tm(0, d, ctx_mine, ctx_ref.at[tm]),
            to_tm(1, d, cols_mine.at[lax.rem(tm + d, tms)], cols_ref.at[tm]),
        )
    ]
    own_grad = pltpu.make_async_copy(wgrad_ref, grads.at[st], keep.at[0])
    own_ctx = pltpu.make_async_copy(ctx_mine, ctx_ref.at[tm], keep.at[1])
    own_cols = pltpu.make_async_copy(cols_mine.at[tm], cols_ref.at[tm], keep.at[2])
    edge = pltpu.make_async_copy(sig.at[pl.ds(0, tile)], edge_hbm, keep.at[3])

    lens_ref[st] = jnp.full(lens_ref.shape[1:], len_ref[0], jnp.int32)
    length = len_ref[0]

    def chunk(token):
        base = token * POOL
        past = sig[pl.ds(base, POOL), :]
        cur = sig[pl.ds(base + tile, POOL), :]
        mixed_f = jnp.dot(past, w_ref[:chans, :chans], preferred_element_type=F32)
        mixed_f += jnp.dot(cur, w_ref[chans:, :chans], preferred_element_type=F32)
        mixed_g = jnp.dot(past, gate_w[:chans], preferred_element_type=F32)
        mixed_g += jnp.dot(cur, gate_w[chans:], preferred_element_type=F32)
        row = lax.broadcasted_iota(jnp.int32, (POOL, 128), 0) + (tm * samples + base)
        half = jnp.where(row < length, 0.5, 0.0)
        half = jnp.concatenate([half] * (chans // 128), axis=1)
        t = jnp.tanh(mixed_f)
        s = half * jnp.tanh(mixed_g) + half
        h = t * s
        a_buf[pl.ds(base, POOL), :chans] = (s - t * h).astype(BF16)
        a_buf[pl.ds(base, POOL), chans:] = (h - h * s).astype(BF16)
        hs = jnp.sum(h, axis=0, keepdims=True)
        ss = jnp.sum(cur.astype(F32) * half, axis=0, keepdims=True) * 2.0
        return hs, ss

    def body(it, carry):
        r = rounds - 1 - it
        per_tile = tile // POOL
        rows = [None] * (group * per_tile)
        for k in reversed(range(group)):
            i = r * group + k
            if k > 0:
                load(i - 1).wait()
            else:

                @pl.when(r > 0)
                def _():
                    load(i - 1).wait()

                @pl.when((r == 0) & (tm > 0))
                def _():
                    halo.wait_recv()

                @pl.when((r == 0) & (tm == 0))
                def _():
                    sig[pl.ds(0, tile), :] = jnp.zeros((tile, chans), BF16)

            for j in range(per_tile):
                rows[k * per_tile + j] = chunk(i * per_tile + j)
            save(i).start()
        block = pl.ds(pl.multiple_of(r * group * per_tile, 8), group * per_tile)
        hsum_ref[block, :] = jnp.concatenate([a for a, _ in rows], axis=0)
        sums[block, :] = jnp.concatenate([b for _, b in rows], axis=0)

        @pl.when(it == 0)
        def _():
            pl.semaphore_wait(barrier, others - 1 + chips)

            @pl.when(tm < tms - 1)
            def _():
                halo.start()
            own_grad.start()
            for copy in grad_copies:
                copy.start()

        @pl.when(it == 1)
        def _():
            own_grad.wait()
            for copy in grad_copies:
                copy.wait()
            for p in range(parts):
                ctx_mine[p] = lax.dot_general(
                    grads[p], wout_ref[...], (((1,), (1,)), ((), ())), preferred_element_type=F32
                ).astype(BF16)
                for k in range(tms):
                    cols_mine[k, p] = grads[p, :, k * columns : (k + 1) * columns]
            own_ctx.start()
            own_cols.start()
            for copy in tm_copies:
                copy.start()

        return carry

    load(steps - 1).wait()
    lax.fori_loop(0, rounds, body, 0)
    edge.start()

    total = hsum_ref[...]
    high = total.astype(BF16)
    low = (total - high.astype(F32)).astype(BF16)
    resid = jnp.dot(high, wres_ref[...], preferred_element_type=F32)
    resid += jnp.dot(low, wres_ref[...], preferred_element_type=F32)
    pool_ref[st, tm] = ((sums[...] + resid) / POOL).astype(BF16)

    def spread(d):
        return pltpu.make_async_remote_copy(
            src_ref=pool_ref.at[st, tm],
            dst_ref=pool_ref.at[st, tm],
            send_sem=send_pool.at[d],
            recv_sem=recv_pool.at[d],
            device_id=peer_of(lax.rem(mine + d, others)),
            device_id_type=MESH,
        )

    def relay(d):
        flat = lax.rem(mine - d + others, others)
        block = pool_ref.at[lax.rem(flat, chips) * 2 + core, flat // chips]
        return pltpu.make_async_remote_copy(
            src_ref=block,
            dst_ref=block,
            send_sem=send_near.at[d],
            recv_sem=recv_near.at[d],
            device_id={"stream": chip * 2 + 1 - core},
            device_id_type=MESH,
        )

    def launch(d, c):
        spread(d).start()
        return c

    def forward(d, c):
        spread(d).wait_recv()
        relay(d).start()
        return c

    def settle(d, c):
        spread(d).wait_send()
        return c

    def close(d, c):
        relay(d).wait()
        return c

    lax.fori_loop(1, others, launch, 0)
    relay(0).start()
    lax.fori_loop(1, others, forward, 0)
    for copy in tm_copies:
        copy.wait()
    own_ctx.wait()
    own_cols.wait()
    edge.wait()
    for i in range(steps):
        save(i).wait()

    @pl.when(tm < tms - 1)
    def _():
        halo.wait_send()

    lax.fori_loop(1, others, settle, 0)
    lax.fori_loop(0, others, close, 0)


def front(lengths, signal, w_conv, w_out, w_res, d_out, collective):
    samples, chans = signal.shape
    toks, width = d_out.shape
    tms, parts = lax.axis_size("tm"), lax.axis_size("stream")
    steps = samples // DILATION_STEP
    group = 4
    inner = w_out.shape[0]
    others = tms * parts // 2
    columns = width // tms
    anywhere = pl.BlockSpec(memory_space=pl.ANY)
    dma = pltpu.SemaphoreType.DMA
    return pl.pallas_call(
        functools.partial(front_kernel, steps, group),
        out_shape=[
            jax.ShapeDtypeStruct((samples, 2 * chans), BF16),
            jax.ShapeDtypeStruct((DILATION_STEP, chans), BF16),
            jax.ShapeDtypeStruct((toks, chans), F32),
            jax.ShapeDtypeStruct((parts, tms, toks, chans), BF16),
            jax.ShapeDtypeStruct((tms, parts, toks, inner), BF16),
            jax.ShapeDtypeStruct((tms, parts, toks, columns), BF16),
            jax.ShapeDtypeStruct((parts, 8, 128), jnp.int32),
        ],
        in_specs=[pl.BlockSpec(memory_space=pltpu.SMEM), anywhere] + [VMEM_SPEC] * 4,
        out_specs=[anywhere, anywhere] + [VMEM_SPEC] * 5,
        scratch_shapes=[
            pltpu.VMEM((samples + DILATION_STEP, chans), BF16),
            pltpu.VMEM((samples, 2 * chans), BF16),
            pltpu.VMEM((parts, toks, width), BF16),
            pltpu.VMEM((2 * chans, chans), BF16),
            pltpu.VMEM((parts, toks, inner), BF16),
            pltpu.VMEM((tms, parts, toks, columns), BF16),
            pltpu.VMEM((toks, chans), F32),
            dma((steps,)),
            dma((steps,)),
            dma((3, tms - 1)),
            dma((3, tms - 1)),
            dma((2, parts - 1)),
            dma((2, parts - 1)),
            dma((others,)),
            dma((others,)),
            dma((others,)),
            dma((others,)),
            dma((4,)),
        ],
        compiler_params=pltpu.CompilerParams(collective_id=collective, has_side_effects=True),
        name="front",
    )(lengths, signal, w_conv, w_out, w_res, d_out)


def shifted(value, axis, by):
    length = lax.axis_size(axis)
    pairs = [(i, i + by) for i in range(length) if 0 <= i + by < length]
    return lax.ppermute(value, axis, pairs)


def local(signal, lengths, w_conv, w_res, w_in, w_qkv, w_out, d_out):
    stays, samples, chans = signal.shape
    width = w_in.shape[1]
    size = width // HEADS
    heads = w_out.shape[0] // size
    toks = samples // POOL
    tms, parts = lax.axis_size("tm"), lax.axis_size("stream")
    tm = lax.axis_index("tm")
    group = stays * parts
    total = toks * tms
    flat = signal.reshape(samples, chans)
    info = jnp.stack([tm * samples, lengths[0]]).astype(jnp.int32)
    columns = width // tms
    gates, incoming, h_sum, all_pool, all_ctx, all_cols, lens = front(
        lengths, flat, w_conv, w_out, w_res, d_out.reshape(toks, width), 0
    )
    group_len = lens[:, 0, 0]
    own_pool = lax.dynamic_slice_in_dim(all_pool, tm, 1, 1)
    own_pool = lax.dynamic_slice_in_dim(own_pool, lax.axis_index("stream"), 1, 0)
    own_tok = dot("btc,cd->btd", own_pool.reshape(1, toks, chans), w_in).astype(BF16)
    all_pool = all_pool.reshape(group, total, chans)
    all_ctx = all_ctx.transpose(1, 0, 2, 3).reshape(group, total, heads * size)
    all_cols = all_cols.transpose(1, 0, 2, 3).reshape(group, total, columns)
    tok = dot("btc,cd->btd", all_pool, w_in).astype(BF16).astype(F32)
    r = lax.rsqrt(jnp.mean(tok * tok, axis=-1, keepdims=True) + EPS)
    normed = (tok * r).astype(BF16)
    proj = dot("btd,de->bte", normed, w_qkv).astype(BF16)
    context, d_proj = attention(proj, all_ctx, group_len, heads, size)
    own_ctx = lax.dynamic_slice_in_dim(context, tm * toks, toks, 1)
    out_part = dot("bte,ed->btd", own_ctx, w_out).astype(BF16)
    g_out = dot("bte,btd->ed", context, all_cols)
    own_norm = lax.dynamic_slice_in_dim(normed, tm * columns, columns, 2)
    g_qkv = dot("btd,bte->de", own_norm, d_proj)
    d_normed = dot("bte,de->btd", d_proj, w_qkv)
    inner = jnp.sum(d_normed * tok, axis=-1, keepdims=True)
    d_group = (r * d_normed - tok * (r * r * r) * inner / width).astype(BF16)
    own_group = lax.dynamic_slice_in_dim(d_group, tm * toks, toks, 1)
    g_in_part = dot("btc,btd->cd", all_pool, d_group).astype(BF16)
    in_rows = chans // parts
    g_in_cols = dot("btc,btd->cd", all_pool, all_cols)
    stream = lax.axis_index("stream")
    g_in_cols = lax.dynamic_slice_in_dim(g_in_cols, stream * in_rows, in_rows, 0)
    (s_group,) = exchange(
        "stream", 2, [("reduce", own_group.reshape(parts, stays, toks, width))]
    )
    d_tok = (s_group + d_out.astype(F32)).astype(BF16)
    d_pooled = dot("btd,cd->btc", d_tok, w_in)
    d_res16 = (d_pooled / POOL).astype(BF16).reshape(toks, chans)
    g_res = lax.dot_general(h_sum, d_res16.astype(F32), (((0,), (0,)), ((), ())), precision=HIGH)
    d_hidden = lax.dot_general(
        d_res16, w_res, (((1,), (1,)), ((), ())), preferred_element_type=F32
    )
    per_tile = (samples // DILATION_STEP, DILATION_STEP // POOL, chans)
    d_sig, first, g_conv, s_out, s_in = conv_backward(
        info,
        incoming,
        flat,
        gates,
        d_hidden.reshape(per_tile),
        d_res16.astype(F32).reshape(per_tile),
        w_conv,
        "stream",
        8,
        [
            ("reduce", out_part.reshape(parts, stays, toks, width)),
            ("reduce", g_in_part.reshape(parts, in_rows, width)),
        ],
    )
    out = (own_tok.astype(F32) + s_out).astype(BF16)
    arriving = shifted(first, "tm", -1)
    edge = samples - DILATION_STEP
    last = (d_sig[edge:].astype(F32) + arriving.astype(F32)).astype(BF16)
    d_signal = jnp.concatenate([d_sig[:edge], last], axis=0)[None]
    s_conv, s_res = exchange(
        "stream",
        3,
        [
            ("reduceb", g_conv.reshape(parts, -1, 2 * chans)),
            ("reduceb", g_res.astype(BF16).reshape(parts, -1, chans)),
        ],
    )
    a_conv, a_res, a_in = final_sums(
        "tm",
        4,
        s_conv.reshape(tms, -1, 2 * chans),
        s_res.reshape(tms, -1, chans),
        g_in_cols.astype(BF16),
    )
    sum_conv = a_conv.reshape(2 * chans // parts, 2 * chans).astype(F32)
    sum_res = a_res.reshape(chans // parts, chans).astype(F32)
    sum_in = s_in + a_in.transpose(1, 0, 2).reshape(in_rows, width).astype(F32)
    return (out, d_signal, sum_conv, sum_res, sum_in, g_qkv, g_out)


def solution(mesh):
    in_specs = (
        P("stream", "tm", None),
        P("stream"),
        P(),
        P(),
        P(),
        P(None, "stream"),
        P("stream", None),
        P("stream", "tm", None),
    )
    out_specs = (
        P("stream", "tm", None),
        P("stream", "tm", None),
        P("stream", None),
        P("stream", None),
        P("stream", None),
        P("tm", "stream"),
        P("stream", "tm"),
    )
    return jax.shard_map(local, mesh=mesh, in_specs=in_specs, out_specs=out_specs, check_vma=False)
```

```python
import functools
import math

import jax
import jax.numpy as jnp
from jax import lax
from jax.experimental import pallas as pl
from jax.experimental.pallas import tpu as pltpu
from jax.sharding import PartitionSpec as P

HEADS = 16
POOL = 256
DILATION_STEP = 512
EPS = 1e-05
BF16 = jnp.bfloat16
F32 = jnp.float32
MESH = pl.DeviceIdType.MESH
VMEM_SPEC = pl.BlockSpec(memory_space=pltpu.VMEM)


def device_of(tm, stream):
    return {"tm": tm, "stream": stream}


def front_kernel(
    steps, group, len_ref, sig_hbm, w_ref, wout_ref, wres_ref, wgrad_ref,
    a_hbm, edge_hbm, hsum_ref, pool_ref, ctx_ref, cols_ref, lens_ref,
    sig, a_buf, grads, gate_w, ctx_mine, cols_mine, sums, sem_in, sem_out, send_tm, recv_tm,
    send_st, recv_st, send_pool, recv_pool, send_near, recv_near, keep,
):
    tms, parts = lax.axis_size("tm"), lax.axis_size("stream")
    tm, st = lax.axis_index("tm"), lax.axis_index("stream")
    chips = parts // 2
    core, chip = lax.rem(st, 2), st // 2
    mine = tm * chips + chip
    tile = DILATION_STEP
    samples = steps * tile
    chans = w_ref.shape[1] // 2
    toks = samples // POOL
    rounds = steps // group

    def peer_of(flat):
        return device_of(flat // chips, lax.rem(flat, chips) * 2 + core)

    barrier = pltpu.get_barrier_semaphore()

    def greet(device):
        pl.semaphore_signal(barrier, inc=1, device_id=device, device_id_type=MESH)

    others = tms * chips
    lax.fori_loop(1, others, lambda d, c: (greet(peer_of(lax.rem(mine + d, others))), c)[1], 0)
    for d in range(chips):
        greet(device_of(tm, lax.rem(chip + d, chips) * 2 + 1 - core))

    def load(i):
        return pltpu.make_async_copy(
            sig_hbm.at[pl.ds(i * tile, tile)], sig.at[pl.ds((i + 1) * tile, tile)], sem_in.at[i]
        )

    def save(i):
        return pltpu.make_async_copy(
            a_buf.at[pl.ds(i * tile, tile)], a_hbm.at[pl.ds(i * tile, tile)], sem_out.at[i]
        )

    for i in reversed(range(steps)):
        load(i).start()
    gate_w[...] = w_ref[:, chans:] * jnp.asarray(0.5, BF16)

    halo = pltpu.make_async_remote_copy(
        src_ref=sig_hbm.at[pl.ds(samples - tile, tile)],
        dst_ref=sig.at[pl.ds(0, tile)],
        send_sem=send_tm.at[2, 0],
        recv_sem=recv_tm.at[2, 0],
        device_id={"tm": lax.rem(tm + 1, tms)},
        device_id_type=MESH,
    )

    def to_stream(j, d, src, dst):
        return pltpu.make_async_remote_copy(
            src_ref=src,
            dst_ref=dst,
            send_sem=send_st.at[j, d - 1],
            recv_sem=recv_st.at[j, d - 1],
            device_id={"stream": lax.rem(st + d, parts)},
            device_id_type=MESH,
        )

    grad_copies = [
        copy
        for d in range(1, parts)
        for copy in (
            to_stream(0, d, wgrad_ref, grads.at[st]),
            to_stream(1, d, lens_ref.at[st], lens_ref.at[st]),
        )
    ]

    def to_tm(j, d, src, dst):
        return pltpu.make_async_remote_copy(
            src_ref=src,
            dst_ref=dst,
            send_sem=send_tm.at[j, d - 1],
            recv_sem=recv_tm.at[j, d - 1],
            device_id={"tm": lax.rem(tm + d, tms)},
            device_id_type=MESH,
        )

    width = grads.shape[2]
    columns = width // tms

    tm_copies = [
        copy
        for d in range(1, tms)
        for copy in (
            to_tm(0, d, ctx_mine, ctx_ref.at[tm]),
            to_tm(1, d, cols_mine.at[lax.rem(tm + d, tms)], cols_ref.at[tm]),
        )
    ]
    own_grad = pltpu.make_async_copy(wgrad_ref, grads.at[st], keep.at[0])
    own_ctx = pltpu.make_async_copy(ctx_mine, ctx_ref.at[tm], keep.at[1])
    own_cols = pltpu.make_async_copy(cols_mine.at[tm], cols_ref.at[tm], keep.at[2])
    edge = pltpu.make_async_copy(sig.at[pl.ds(0, tile)], edge_hbm, keep.at[3])

    lens_ref[st] = jnp.full(lens_ref.shape[1:], len_ref[0], jnp.int32)
    length = len_ref[0]

    def chunk(token):
        base = token * POOL
        past = sig[pl.ds(base, POOL), :]
        cur = sig[pl.ds(base + tile, POOL), :]
        mixed_f = jnp.dot(past, w_ref[:chans, :chans], preferred_element_type=F32)
        mixed_f += jnp.dot(cur, w_ref[chans:, :chans], preferred_element_type=F32)
        mixed_g = jnp.dot(past, gate_w[:chans], preferred_element_type=F32)
        mixed_g += jnp.dot(cur, gate_w[chans:], preferred_element_type=F32)
        row = lax.broadcasted_iota(jnp.int32, (POOL, 128), 0) + (tm * samples + base)
        half = jnp.where(row < length, 0.5, 0.0)
        half = jnp.concatenate([half] * (chans // 128), axis=1)
        t = jnp.tanh(mixed_f)
        s = half * jnp.tanh(mixed_g) + half
        h = t * s
        a_buf[pl.ds(base, POOL), :chans] = (s - t * h).astype(BF16)
        a_buf[pl.ds(base, POOL), chans:] = (h - h * s).astype(BF16)
        hs = jnp.sum(h, axis=0, keepdims=True)
        ss = jnp.sum(cur.astype(F32) * half, axis=0, keepdims=True) * 2.0
        return hs, ss

    def body(it, carry):
        r = rounds - 1 - it
        per_tile = tile // POOL
        rows = [None] * (group * per_tile)
        for k in reversed(range(group)):
            i = r * group + k
            if k > 0:
                load(i - 1).wait()
            else:

                @pl.when(r > 0)
                def _():
                    load(i - 1).wait()

                @pl.when((r == 0) & (tm > 0))
                def _():
                    halo.wait_recv()

                @pl.when((r == 0) & (tm == 0))
                def _():
                    sig[pl.ds(0, tile), :] = jnp.zeros((tile, chans), BF16)

            for j in range(per_tile):
                rows[k * per_tile + j] = chunk(i * per_tile + j)
            save(i).start()
        block = pl.ds(pl.multiple_of(r * group * per_tile, 8), group * per_tile)
        hsum_ref[block, :] = jnp.concatenate([a for a, _ in rows], axis=0)
        sums[block, :] = jnp.concatenate([b for _, b in rows], axis=0)

        @pl.when(it == 0)
        def _():
            pl.semaphore_wait(barrier, others - 1 + chips)

            @pl.when(tm < tms - 1)
            def _():
                halo.start()
            own_grad.start()
            for copy in grad_copies:
                copy.start()

        @pl.when(it == 1)
        def _():
            own_grad.wait()
            for copy in grad_copies:
                copy.wait()
            for p in range(parts):
                ctx_mine[p] = lax.dot_general(
                    grads[p], wout_ref[...], (((1,), (1,)), ((), ())), preferred_element_type=F32
                ).astype(BF16)
                for k in range(tms):
                    cols_mine[k, p] = grads[p, :, k * columns : (k + 1) * columns]
            own_ctx.start()
            own_cols.start()
            for copy in tm_copies:
                copy.start()

        return carry

    load(steps - 1).wait()
    lax.fori_loop(0, rounds, body, 0)
    edge.start()

    total = hsum_ref[...]
    high = total.astype(BF16)
    low = (total - high.astype(F32)).astype(BF16)
    resid = jnp.dot(high, wres_ref[...], preferred_element_type=F32)
    resid += jnp.dot(low, wres_ref[...], preferred_element_type=F32)
    pool_ref[st, tm] = ((sums[...] + resid) / POOL).astype(BF16)

    def spread(d):
        return pltpu.make_async_remote_copy(
            src_ref=pool_ref.at[st, tm],
            dst_ref=pool_ref.at[st, tm],
            send_sem=send_pool.at[d],
            recv_sem=recv_pool.at[d],
            device_id=peer_of(lax.rem(mine + d, others)),
            device_id_type=MESH,
        )

    def relay(d):
        flat = lax.rem(mine - d + others, others)
        block = pool_ref.at[lax.rem(flat, chips) * 2 + core, flat // chips]
        return pltpu.make_async_remote_copy(
            src_ref=block,
            dst_ref=block,
            send_sem=send_near.at[d],
            recv_sem=recv_near.at[d],
            device_id={"stream": chip * 2 + 1 - core},
            device_id_type=MESH,
        )

    def launch(d, c):
        spread(d).start()
        return c

    def forward(d, c):
        spread(d).wait_recv()
        relay(d).start()
        return c

    def settle(d, c):
        spread(d).wait_send()
        return c

    def close(d, c):
        relay(d).wait()
        return c

    lax.fori_loop(1, others, launch, 0)
    relay(0).start()
    lax.fori_loop(1, others, forward, 0)
    for copy in tm_copies:
        copy.wait()
    own_ctx.wait()
    own_cols.wait()
    edge.wait()
    for i in range(steps):
        save(i).wait()

    @pl.when(tm < tms - 1)
    def _():
        halo.wait_send()

    lax.fori_loop(1, others, settle, 0)
    lax.fori_loop(0, others, close, 0)


def front(lengths, signal, w_conv, w_out, w_res, d_out, collective):
    samples, chans = signal.shape
    toks, width = d_out.shape
    tms, parts = lax.axis_size("tm"), lax.axis_size("stream")
    steps = samples // DILATION_STEP
    group = 4
    inner = w_out.shape[0]
    others = tms * parts // 2
    columns = width // tms
    anywhere = pl.BlockSpec(memory_space=pl.ANY)
    dma = pltpu.SemaphoreType.DMA
    return pl.pallas_call(
        functools.partial(front_kernel, steps, group),
        out_shape=[
            jax.ShapeDtypeStruct((samples, 2 * chans), BF16),
            jax.ShapeDtypeStruct((DILATION_STEP, chans), BF16),
            jax.ShapeDtypeStruct((toks, chans), F32),
            jax.ShapeDtypeStruct((parts, tms, toks, chans), BF16),
            jax.ShapeDtypeStruct((tms, parts, toks, inner), BF16),
            jax.ShapeDtypeStruct((tms, parts, toks, columns), BF16),
            jax.ShapeDtypeStruct((parts, 8, 128), jnp.int32),
        ],
        in_specs=[pl.BlockSpec(memory_space=pltpu.SMEM), anywhere] + [VMEM_SPEC] * 4,
        out_specs=[anywhere, anywhere] + [VMEM_SPEC] * 5,
        scratch_shapes=[
            pltpu.VMEM((samples + DILATION_STEP, chans), BF16),
            pltpu.VMEM((samples, 2 * chans), BF16),
            pltpu.VMEM((parts, toks, width), BF16),
            pltpu.VMEM((2 * chans, chans), BF16),
            pltpu.VMEM((parts, toks, inner), BF16),
            pltpu.VMEM((tms, parts, toks, columns), BF16),
            pltpu.VMEM((toks, chans), F32),
            dma((steps,)),
            dma((steps,)),
            dma((3, tms - 1)),
            dma((3, tms - 1)),
            dma((2, parts - 1)),
            dma((2, parts - 1)),
            dma((others,)),
            dma((others,)),
            dma((others,)),
            dma((others,)),
            dma((4,)),
        ],
        compiler_params=pltpu.CompilerParams(collective_id=collective, has_side_effects=True),
        name="front",
    )(lengths, signal, w_conv, w_out, w_res, d_out)


NT = (((1,), (1,)), ((), ()))
TN = (((0,), (0,)), ((), ()))


def fdot(a, b, dims=(((1,), (0,)), ((), ()))):
    return lax.dot_general(a, b, dims, preferred_element_type=F32)


def attend(heads, size, allowed, proj, dctx, ctx, dproj):
    scale = 1.0 / math.sqrt(size)
    span = range(heads)

    def part(h, j):
        base = (3 * h + j) * size
        return proj[:, base : base + size]

    inner = [slice(h * size, (h + 1) * size) for h in span]
    scores = [fdot(part(h, 0), part(h, 1), NT) * scale for h in span]
    d_prob = [fdot(dctx[:, inner[h]], part(h, 2), NT) for h in span]
    scores = [jnp.where(allowed, a, -1e30) for a in scores]
    weights = [jnp.exp(a - jnp.max(a, axis=-1, keepdims=True)) for a in scores]
    prob = [a * (1.0 / jnp.sum(a, axis=-1, keepdims=True)) for a in weights]
    prob16 = [a.astype(BF16) for a in prob]
    d_score = [
        (p * (d - jnp.sum(d * p, axis=-1, keepdims=True))).astype(BF16)
        for p, d in zip(prob, d_prob)
    ]
    for h in span:
        base = 3 * h * size
        ctx[:, inner[h]] = fdot(prob16[h], part(h, 2))
        d_query = scale * fdot(d_score[h], part(h, 1))
        d_key = scale * fdot(d_score[h], part(h, 0), TN)
        d_value = fdot(prob16[h], dctx[:, inner[h]], TN)
        dproj[:, base : base + size] = d_query.astype(BF16)
        dproj[:, base + size : base + 2 * size] = d_key.astype(BF16)
        dproj[:, base + 2 * size : base + 3 * size] = d_value.astype(BF16)


def back_kernel(
    steps, heads, len_ref, lens_ref, sig_hbm, edge_hbm, a_hbm, hsum_ref, pool_ref, ctx_in, cols_in,
    w_ref, wres_ref, win_ref, wqkv_ref, wout_ref, grad_ref,
    out_ref, dsig_hbm, gconv_ref, gres_ref, gin_ref, gqkv_ref, gout_ref,
    sig, a_buf, dsig, first, arrive, pool_f, pool_b, dctx_f, dctx_b, cols_f, cols_b, tok_v, norm,
    proj, ctx_v, dproj, dg, gin_acc, cols_acc, own_send, own_land, out_send, out_land, cols_mine,
    cols_land, in_parts, in_near, in_sum, in_far, conv_acc, conv_parts, conv_near, conv_sum,
    conv_far, conv_f, conv_rows, conv_rland, conv_own, conv_land, res_acc, res_parts, res_near,
    res_sum, res_far, res_f, res_rows, res_rland, res_own, res_land, dh8, dr8,
    sem_in, sem_a, sem_out, send, recv,
):
    tms, parts = lax.axis_size("tm"), lax.axis_size("stream")
    tm, st = lax.axis_index("tm"), lax.axis_index("stream")
    chips = parts // 2
    core, chip = lax.rem(st, 2), st // 2
    tile = DILATION_STEP
    samples = steps * tile
    chans = w_ref.shape[1] // 2
    toks, width = grad_ref.shape
    total = tms * toks
    inner = wout_ref.shape[0]
    size = inner // heads
    columns = width // tms
    in_rows = chans // parts

    barrier = pltpu.get_barrier_semaphore()
    for d in range(1, parts):
        pl.semaphore_signal(
            barrier, inc=1, device_id={"stream": lax.rem(st + d, parts)}, device_id_type=MESH
        )
    for d in range(1, tms):
        pl.semaphore_signal(
            barrier, inc=1, device_id={"tm": lax.rem(tm + d, tms)}, device_id_type=MESH
        )

    loads = [pltpu.make_async_copy(edge_hbm, sig.at[pl.ds(0, tile)], sem_in.at[0])]
    loads.append(pltpu.make_async_copy(sig_hbm, sig.at[pl.ds(tile, samples)], sem_in.at[1]))
    loads.append(pltpu.make_async_copy(a_hbm, a_buf, sem_a.at[0]))
    for copy in loads:
        copy.start()

    count = iter(range(send.shape[0]))

    def remote(src, dst, device):
        j = next(count)
        return pltpu.make_async_remote_copy(
            src_ref=src,
            dst_ref=dst,
            send_sem=send.at[j],
            recv_sem=recv.at[j],
            device_id=device,
            device_id_type=MESH,
        )

    def to_stream(d):
        return {"stream": lax.rem(st + d, parts)}

    def to_tm(d):
        return {"tm": lax.rem(tm + d, tms)}

    def to_chip(d):
        return {"stream": lax.rem(chip + d, chips) * 2 + core}

    near = {"stream": chip * 2 + 1 - core}

    def begin(copies):
        for copy in copies:
            copy.start()

    def finish(copies):
        for copy in copies:
            copy.wait()

    row = lax.broadcasted_iota(jnp.int32, (total, total), 0)
    col = lax.broadcasted_iota(jnp.int32, (total, total), 1)
    gout_ref[...] = jnp.zeros_like(gout_ref)
    gqkv_ref[...] = jnp.zeros_like(gqkv_ref)
    gin_acc[...] = jnp.zeros_like(gin_acc)
    cols_acc[...] = jnp.zeros_like(cols_acc)
    mine = pl.ds(pl.multiple_of(tm * toks, 8), toks)

    def stay(s, carry):
        for k in range(tms):
            rows = slice(k * toks, (k + 1) * toks)
            pool_f[rows, :] = pool_ref[s, k].astype(F32)
            dctx_f[rows, :] = ctx_in[k, s].astype(F32)
            cols_f[rows, :] = cols_in[k, s].astype(F32)
        pool_b[...] = pool_f[...].astype(BF16)
        dctx_b[...] = dctx_f[...].astype(BF16)
        cols_b[...] = cols_f[...].astype(BF16)
        tok = fdot(pool_b[...], win_ref[...]).astype(BF16).astype(F32)
        tok_v[...] = tok
        r = lax.rsqrt(jnp.mean(tok * tok, axis=-1, keepdims=True) + EPS)
        norm[...] = (tok * r).astype(BF16)
        proj[...] = fdot(norm[...], wqkv_ref[...]).astype(BF16)
        limit = lens_ref[s, 0:1, 0:1]
        allowed = (col <= row) & (col * POOL < limit)
        attend(heads, size, allowed, proj, dctx_b, ctx_v, dproj)
        context = ctx_v[...].astype(BF16)
        gout_ref[...] += fdot(context, cols_b[...], TN)
        cols_acc[...] += fdot(pool_b[...], cols_b[...], TN)
        if columns % 128 == 0:
            own = norm[:, pl.ds(pl.multiple_of(tm * columns, columns), columns)]
            gqkv_ref[...] += fdot(own, dproj[...], TN)
        else:
            for k in range(tms):

                @pl.when(tm == k)
                def _():
                    own = norm[:, k * columns : (k + 1) * columns]
                    gqkv_ref[...] += fdot(own, dproj[...], TN)

        d_normed = fdot(dproj[...], wqkv_ref[...], NT)
        tok = tok_v[...]
        along = jnp.sum(d_normed * tok, axis=-1, keepdims=True)
        d_group = r * d_normed - tok * (r * r * r * along / width)
        dg[...] = d_group
        own_send[s] = dg[mine, :].astype(BF16)
        out_send[s] = fdot(ctx_v[mine, :].astype(BF16), wout_ref[...]).astype(BF16)
        gin_acc[...] += fdot(pool_b[...], d_group.astype(BF16), TN)
        return carry

    lax.fori_loop(0, parts, stay, 0)

    own_copies = [
        remote(own_send.at[lax.rem(st + d, parts)], own_land.at[d - 1], to_stream(d))
        for d in range(1, parts)
    ]
    out_copies = [
        remote(out_send.at[lax.rem(st + d, parts)], out_land.at[d - 1], to_stream(d))
        for d in range(1, parts)
    ]
    cols_copies = [remote(cols_mine, cols_land.at[tm], to_tm(d)) for d in range(1, tms)]
    back = remote(first, arrive, {"tm": lax.rem(tm + tms - 1, tms)})

    def reduce_near(blocks, land):
        return [remote(blocks.at[1 - core], land, near)]

    def reduce_far(sums, land):
        return [
            remote(sums.at[lax.rem(chip + d, chips)], land.at[d - 1], to_chip(d))
            for d in range(1, chips)
        ]

    in_one = reduce_near(in_parts, in_near)
    in_two = reduce_far(in_sum, in_far)
    conv_one = reduce_near(conv_parts, conv_near) + reduce_near(res_parts, res_near)
    conv_two = reduce_far(conv_sum, conv_far) + reduce_far(res_sum, res_far)
    conv_three = [
        copy
        for d in range(1, tms)
        for copy in (
            remote(conv_rows.at[lax.rem(tm + d, tms)], conv_rland.at[d - 1], to_tm(d)),
            remote(res_rows.at[lax.rem(tm + d, tms)], res_rland.at[d - 1], to_tm(d)),
        )
    ]
    conv_four = [
        copy
        for d in range(1, tms)
        for copy in (
            remote(conv_own, conv_land.at[tm], to_tm(d)),
            remote(res_own, res_land.at[tm], to_tm(d)),
        )
    ]

    def split(acc, blocks):
        rows = blocks.shape[2]
        for c in range(2):
            for q in range(chips):
                base = (q * 2 + c) * rows
                blocks[c, q] = acc[base : base + rows, :].astype(BF16)

    def add_near(blocks, land, sums):
        for q in range(chips):
            sums[q] = (blocks[core, q].astype(F32) + land[q].astype(F32)).astype(BF16)

    def add_far(sums, land):
        value = sums[chip].astype(F32)
        for d in range(1, chips):
            value += land[d - 1].astype(F32)
        return value

    def cut(value, full, rows):
        full[...] = value
        n = rows.shape[1]
        for k in range(tms):
            rows[k] = full[k * n : (k + 1) * n, :].astype(BF16)

    def add_rows(rows, land, own, gathered):
        value = rows[tm].astype(F32)
        for d in range(1, tms):
            value += land[d - 1].astype(F32)
        own[...] = value.astype(BF16)
        gathered[tm] = value.astype(BF16)

    pl.semaphore_wait(barrier, parts - 1 + tms - 1)
    begin(own_copies)
    split(gin_acc, in_parts)
    cols_mine[...] = cols_acc[pl.ds(pl.multiple_of(st * in_rows, 8), in_rows), :].astype(BF16)
    cols_land[tm] = cols_mine[...]
    begin(in_one)
    begin(out_copies)
    begin(cols_copies)
    own_tok = fdot(pool_ref[st, tm], win_ref[...]).astype(BF16).astype(F32)

    finish(own_copies)
    d_tok = own_send[st].astype(F32) + grad_ref[...].astype(F32)
    for d in range(1, parts):
        d_tok += own_land[d - 1].astype(F32)
    d_pooled = fdot(d_tok.astype(BF16), win_ref[...], NT)
    d_res = (d_pooled / POOL).astype(BF16)
    d_hidden = fdot(d_res, wres_ref[...], NT)
    d_resf = d_res.astype(F32)
    for t in range(toks):
        dh8[t] = jnp.broadcast_to(d_hidden[t : t + 1, :], (8, chans))
        dr8[t] = jnp.broadcast_to(d_resf[t : t + 1, :], (8, chans))
    high = hsum_ref[...].astype(BF16)
    low = (hsum_ref[...] - high.astype(F32)).astype(BF16)
    res_acc[...] = fdot(high, d_res, TN) + fdot(low, d_res, TN)
    split(res_acc, res_parts)

    finish(in_one)
    add_near(in_parts, in_near, in_sum)
    begin(in_two)
    finish(loads)

    per_tile = tile // POOL

    def later_of(i):
        return fdot(a_buf[pl.ds(i * tile, tile), :], w_ref[:chans, :], NT).astype(BF16)

    conv_acc[...] = jnp.zeros_like(conv_acc)

    def weigh(i, carry):
        rows = pl.ds(i * tile, tile)
        for j in range(per_tile):
            token = i * per_tile + j
            base = pl.ds(token * POOL, POOL)
            gate = dh8[token]
            for c in range(2):
                lanes = slice(c * chans, (c + 1) * chans)
                a = a_buf[base, lanes].astype(F32).reshape(POOL // 8, 8, chans)
                a_buf[base, lanes] = (a * gate[None]).reshape(POOL, chans).astype(BF16)
        dm = a_buf[rows, :]
        conv_acc[:chans, :] += fdot(sig[rows, :], dm, TN)
        conv_acc[chans:, :] += fdot(sig[pl.ds((i + 1) * tile, tile), :], dm, TN)

        @pl.when(i == 0)
        def _():
            first[...] = later_of(0)

            @pl.when(tm > 0)
            def _():
                back.start()

        return carry

    lax.fori_loop(0, steps, weigh, 0)

    split(conv_acc, conv_parts)
    begin(conv_one)

    length = len_ref[0]

    def emit(i, later):
        rows = pl.ds(i * tile, tile)
        here = fdot(a_buf[rows, :], w_ref[chans:, :], NT)
        for j in range(per_tile):
            token = i * per_tile + j
            index = lax.broadcasted_iota(jnp.int32, (POOL, 128), 0) + (tm * samples + token * POOL)
            valid = jnp.where(index < length, 1.0, 0.0)
            valid = jnp.concatenate([valid] * (chans // 128), axis=1)
            own = dr8[token][None] * valid.reshape(POOL // 8, 8, chans)
            part = slice(j * POOL, (j + 1) * POOL)
            value = own.reshape(POOL, chans) + here[part] + later[part].astype(F32)
            dsig[pl.ds(token * POOL, POOL), :] = value.astype(BF16)
        pltpu.make_async_copy(dsig.at[rows], dsig_hbm.at[rows], sem_out.at[i]).start()

    def emit_step(i, carry):
        emit(i, later_of(i + 1))
        return carry

    cuts = [0, steps // 6, steps // 2, steps - 1]
    lax.fori_loop(cuts[0], cuts[1], emit_step, 0)
    finish(conv_one)
    add_near(conv_parts, conv_near, conv_sum)
    add_near(res_parts, res_near, res_sum)
    begin(conv_two)
    lax.fori_loop(cuts[1], cuts[2], emit_step, 0)
    finish(in_two)
    finish(conv_two)
    cut(add_far(conv_sum, conv_far), conv_f, conv_rows)
    cut(add_far(res_sum, res_far), res_f, res_rows)
    begin(conv_three)
    lax.fori_loop(cuts[2], cuts[3], emit_step, 0)

    @pl.when(tm < tms - 1)
    def _():
        back.wait_recv()

    @pl.when(tm == tms - 1)
    def _():
        arrive[...] = jnp.zeros_like(arrive)

    emit(steps - 1, arrive[...])
    finish(out_copies)
    value = own_tok + out_send[st].astype(F32)
    for d in range(1, parts):
        value += out_land[d - 1].astype(F32)
    out_ref[...] = value.astype(BF16)
    finish(cols_copies)
    total_in = add_far(in_sum, in_far)
    for k in range(tms):
        lanes = slice(k * columns, (k + 1) * columns)
        gin_ref[:, lanes] = total_in[:, lanes] + cols_land[k].astype(F32)

    finish(conv_three)
    add_rows(conv_rows, conv_rland, conv_own, conv_land)
    add_rows(res_rows, res_rland, res_own, res_land)
    begin(conv_four)

    @pl.when(tm > 0)
    def _():
        back.wait_send()

    for i in range(steps):
        rows = pl.ds(i * tile, tile)
        pltpu.make_async_copy(dsig.at[rows], dsig_hbm.at[rows], sem_out.at[i]).wait()
    finish(conv_four)
    for k in range(tms):
        n = conv_land.shape[1]
        gconv_ref[k * n : (k + 1) * n, :] = conv_land[k].astype(F32)
        n = res_land.shape[1]
        gres_ref[k * n : (k + 1) * n, :] = res_land[k].astype(F32)


def back(lengths, lens, signal, edge, gates, hsum, pool, ctx, cols, weights, d_out, heads, collective):
    w_conv, w_res, w_in, w_qkv, w_out = weights
    samples, chans = signal.shape
    toks, width = d_out.shape
    tms, parts = lax.axis_size("tm"), lax.axis_size("stream")
    chips = parts // 2
    steps = samples // DILATION_STEP
    total = toks * tms
    inner = w_out.shape[0]
    triple = w_qkv.shape[1]
    columns = width // tms
    joined = 2 * chans
    conv_n, res_n = joined // parts, chans // parts
    anywhere = pl.BlockSpec(memory_space=pl.ANY)
    dma = pltpu.SemaphoreType.DMA

    def vm(*shape, dtype=BF16):
        return pltpu.VMEM(shape, dtype)

    def reduction(rows, n, lanes):
        return [
            vm(rows, lanes, dtype=F32),
            vm(2, chips, n, lanes),
            vm(chips, n, lanes),
            vm(chips, n, lanes),
            vm(max(chips - 1, 1), n, lanes),
            vm(n, lanes, dtype=F32),
            vm(tms, n // tms, lanes),
            vm(tms - 1, n // tms, lanes),
            vm(n // tms, lanes),
            vm(tms, n // tms, lanes),
        ]

    copies = 2 * (parts - 1) + 5 * (tms - 1) + 1 + 3 + 3 * (chips - 1)
    return pl.pallas_call(
        functools.partial(back_kernel, steps, heads),
        out_shape=[
            jax.ShapeDtypeStruct((toks, width), BF16),
            jax.ShapeDtypeStruct((samples, chans), BF16),
            jax.ShapeDtypeStruct((conv_n, joined), F32),
            jax.ShapeDtypeStruct((res_n, chans), F32),
            jax.ShapeDtypeStruct((res_n, width), F32),
            jax.ShapeDtypeStruct((columns, triple), F32),
            jax.ShapeDtypeStruct((inner, columns), F32),
        ],
        in_specs=[pl.BlockSpec(memory_space=pltpu.SMEM), VMEM_SPEC, anywhere, anywhere, anywhere]
        + [VMEM_SPEC] * 10,
        out_specs=[VMEM_SPEC, anywhere] + [VMEM_SPEC] * 5,
        scratch_shapes=[
            vm(samples + DILATION_STEP, chans),
            vm(samples, joined),
            vm(samples, chans),
            vm(DILATION_STEP, chans),
            vm(DILATION_STEP, chans),
            vm(total, chans, dtype=F32),
            vm(total, chans),
            vm(total, inner, dtype=F32),
            vm(total, inner),
            vm(total, columns, dtype=F32),
            vm(total, columns),
            vm(total, width, dtype=F32),
            vm(total, width),
            vm(total, triple),
            vm(total, inner, dtype=F32),
            vm(total, triple),
            vm(total, width, dtype=F32),
            vm(chans, width, dtype=F32),
            vm(chans, columns, dtype=F32),
            vm(parts, toks, width),
            vm(parts - 1, toks, width),
            vm(parts, toks, width),
            vm(parts - 1, toks, width),
            vm(res_n, columns),
            vm(tms, res_n, columns),
            vm(2, chips, res_n, width),
            vm(chips, res_n, width),
            vm(chips, res_n, width),
            vm(max(chips - 1, 1), res_n, width),
        ]
        + reduction(joined, conv_n, joined)
        + reduction(chans, res_n, chans)
        + [
            vm(toks, 8, chans, dtype=F32),
            vm(toks, 8, chans, dtype=F32),
            dma((2,)),
            dma((1,)),
            dma((steps,)),
            dma((copies,)),
            dma((copies,)),
        ],
        compiler_params=pltpu.CompilerParams(
            collective_id=collective, has_side_effects=True, vmem_limit_bytes=60 * 1024 * 1024
        ),
        name="back",
    )(lengths, lens, signal, edge, gates, hsum, pool, ctx, cols, w_conv, w_res, w_in, w_qkv, w_out, d_out)


def local(signal, lengths, w_conv, w_res, w_in, w_qkv, w_out, d_out):
    samples, chans = signal.shape[1:]
    toks, width = d_out.shape[1:]
    flat, grad = signal.reshape(samples, chans), d_out.reshape(toks, width)
    heads = w_out.shape[0] // (width // HEADS)
    gates, edge, hsum, pool, ctx, cols, lens = front(
        lengths, flat, w_conv, w_out, w_res, grad, 0
    )
    weights = (w_conv, w_res, w_in, w_qkv, w_out)
    out, d_sig, *grads = back(
        lengths, lens, flat, edge, gates, hsum, pool, ctx, cols, weights, grad, heads, 1
    )
    return (out[None], d_sig[None], *grads)


def solution(mesh):
    in_specs = (
        P("stream", "tm", None),
        P("stream"),
        P(),
        P(),
        P(),
        P(None, "stream"),
        P("stream", None),
        P("stream", "tm", None),
    )
    out_specs = (
        P("stream", "tm", None),
        P("stream", "tm", None),
        P("stream", None),
        P("stream", None),
        P("stream", None),
        P("tm", "stream"),
        P("stream", "tm"),
    )
    return jax.shard_map(local, mesh=mesh, in_specs=in_specs, out_specs=out_specs, check_vma=False)
```

```python
import functools
import math

import jax
import jax.numpy as jnp
from jax import lax
from jax.experimental import pallas as pl
from jax.experimental.pallas import tpu as pltpu
from jax.sharding import PartitionSpec as P

HEADS = 16
POOL = 256
DILATION_STEP = 512
EPS = 1e-05
BF16 = jnp.bfloat16
F32 = jnp.float32
MESH = pl.DeviceIdType.MESH
VMEM_SPEC = pl.BlockSpec(memory_space=pltpu.VMEM)


def device_of(tm, stream):
    return {"tm": tm, "stream": stream}


def front_kernel(
    steps, group, len_ref, sig_hbm, wqkv_hbm, w_ref, wout_ref, wres_ref, wgrad_ref,
    a_hbm, edge_hbm, hsum_ref, pool_ref, ctx_ref, cols_ref, lens_ref, wt_ref, wqkvt_ref,
    sig, a_buf, grads, grads_f, wqkv, gate_w, ctx_mine, cols_mine, sums, sem_in, sem_out, send_tm, recv_tm,
    send_st, recv_st, send_pool, recv_pool, send_near, recv_near, keep,
):
    tms, parts = lax.axis_size("tm"), lax.axis_size("stream")
    tm, st = lax.axis_index("tm"), lax.axis_index("stream")
    chips = parts // 2
    core, chip = lax.rem(st, 2), st // 2
    mine = tm * chips + chip
    tile = DILATION_STEP
    samples = steps * tile
    chans = w_ref.shape[1] // 2
    toks = samples // POOL
    rounds = steps // group

    def peer_of(flat):
        return device_of(flat // chips, lax.rem(flat, chips) * 2 + core)

    barrier = pltpu.get_barrier_semaphore()

    def greet(device):
        pl.semaphore_signal(barrier, inc=1, device_id=device, device_id_type=MESH)

    others = tms * chips
    lax.fori_loop(1, others, lambda d, c: (greet(peer_of(lax.rem(mine + d, others))), c)[1], 0)
    for d in range(chips):
        greet(device_of(tm, lax.rem(chip + d, chips) * 2 + 1 - core))

    def load(i):
        return pltpu.make_async_copy(
            sig_hbm.at[pl.ds(i * tile, tile)], sig.at[pl.ds((i + 1) * tile, tile)], sem_in.at[i]
        )

    def save(i):
        return pltpu.make_async_copy(
            a_buf.at[pl.ds(i * tile, tile)], a_hbm.at[pl.ds(i * tile, tile)], sem_out.at[i]
        )

    for i in reversed(range(steps)):
        load(i).start()
    fetch = pltpu.make_async_copy(wqkv_hbm, wqkv, keep.at[4])
    fetch.start()
    gate_w[...] = w_ref[:, chans:] * jnp.asarray(0.5, BF16)

    halo = pltpu.make_async_remote_copy(
        src_ref=sig_hbm.at[pl.ds(samples - tile, tile)],
        dst_ref=sig.at[pl.ds(0, tile)],
        send_sem=send_tm.at[2, 0],
        recv_sem=recv_tm.at[2, 0],
        device_id={"tm": lax.rem(tm + 1, tms)},
        device_id_type=MESH,
    )

    def to_stream(j, d, src, dst):
        return pltpu.make_async_remote_copy(
            src_ref=src,
            dst_ref=dst,
            send_sem=send_st.at[j, d - 1],
            recv_sem=recv_st.at[j, d - 1],
            device_id={"stream": lax.rem(st + d, parts)},
            device_id_type=MESH,
        )

    grad_copies = [
        copy
        for d in range(1, parts)
        for copy in (
            to_stream(0, d, wgrad_ref, grads.at[st]),
            to_stream(1, d, lens_ref.at[st], lens_ref.at[st]),
        )
    ]

    def to_tm(j, d, src, dst, device):
        return pltpu.make_async_remote_copy(
            src_ref=src,
            dst_ref=dst,
            send_sem=send_tm.at[j, d - 1],
            recv_sem=recv_tm.at[j, d - 1],
            device_id=device,
            device_id_type=MESH,
        )

    width = grads.shape[2]
    columns = width // tms

    pairs = tms // 2
    across = {"tm": tm + 1 - 2 * lax.rem(tm, 2)}
    ctx_copies = [
        to_tm(0, d, ctx_mine, ctx_ref.at[tm], {"tm": lax.rem(tm + 2 * d, tms)})
        for d in range(1, pairs)
    ]
    ctx_passes = []
    for d in range(pairs):
        block = ctx_ref.at[lax.rem(tm - 2 * d + tms, tms)]
        ctx_passes.append(to_tm(0, pairs + d, block if d else ctx_mine, block, across))
    cols_copies = [
        to_tm(
            1, d, cols_mine.at[lax.rem(tm + d, tms)], cols_ref.at[st, tm],
            {"tm": lax.rem(tm + d, tms)},
        )
        for d in range(1, tms)
    ]
    cols_shares = [to_stream(2, d, cols_ref.at[st], cols_ref.at[st]) for d in range(1, parts)]
    own_grad = pltpu.make_async_copy(wgrad_ref, grads.at[st], keep.at[0])
    own_ctx = pltpu.make_async_copy(ctx_mine, ctx_ref.at[tm], keep.at[1])
    own_cols = pltpu.make_async_copy(cols_mine.at[tm], cols_ref.at[st, tm], keep.at[2])
    edge = pltpu.make_async_copy(sig.at[pl.ds(0, tile)], edge_hbm, keep.at[3])

    for k in range(tms):
        cols_mine[k] = wgrad_ref[:, k * columns : (k + 1) * columns]
    lens_ref[st] = jnp.full(lens_ref.shape[1:], len_ref[0], jnp.int32)
    length = len_ref[0]

    def chunk(token):
        base = token * POOL
        past = sig[pl.ds(base, POOL), :]
        cur = sig[pl.ds(base + tile, POOL), :]
        mixed_f = jnp.dot(past, w_ref[:chans, :chans], preferred_element_type=F32)
        mixed_f += jnp.dot(cur, w_ref[chans:, :chans], preferred_element_type=F32)
        mixed_g = jnp.dot(past, gate_w[:chans], preferred_element_type=F32)
        mixed_g += jnp.dot(cur, gate_w[chans:], preferred_element_type=F32)
        row = lax.broadcasted_iota(jnp.int32, (POOL, 128), 0) + (tm * samples + base)
        half = jnp.where(row < length, 0.5, 0.0)
        half = jnp.concatenate([half] * (chans // 128), axis=1)
        t = jnp.tanh(mixed_f)
        s = half * jnp.tanh(mixed_g) + half
        h = t * s
        a_buf[pl.ds(base, POOL), :chans] = (s - t * h).astype(BF16)
        a_buf[pl.ds(base, POOL), chans:] = (h - h * s).astype(BF16)
        hs = jnp.sum(h, axis=0, keepdims=True)
        ss = jnp.sum(cur.astype(F32) * half, axis=0, keepdims=True) * 2.0
        return hs, ss

    def body(it, carry):
        r = rounds - 1 - it
        per_tile = tile // POOL
        rows = [None] * (group * per_tile)
        for k in reversed(range(group)):
            i = r * group + k
            if k > 0:
                load(i - 1).wait()
            else:

                @pl.when(r > 0)
                def _():
                    load(i - 1).wait()

                @pl.when((r == 0) & (tm > 0))
                def _():
                    halo.wait_recv()

                @pl.when((r == 0) & (tm == 0))
                def _():
                    sig[pl.ds(0, tile), :] = jnp.zeros((tile, chans), BF16)

            for j in range(per_tile):
                rows[k * per_tile + j] = chunk(i * per_tile + j)
            save(i).start()
        block = pl.ds(pl.multiple_of(r * group * per_tile, 8), group * per_tile)
        hsum_ref[block, :] = jnp.concatenate([a for a, _ in rows], axis=0)
        sums[block, :] = jnp.concatenate([b for _, b in rows], axis=0)

        @pl.when(it == 0)
        def _():
            pl.semaphore_wait(barrier, others - 1 + chips)

            @pl.when(tm < tms - 1)
            def _():
                halo.start()
            own_grad.start()
            own_cols.start()
            for copy in grad_copies + cols_copies:
                copy.start()

        @pl.when(it == 1)
        def _():
            own_grad.wait()
            for copy in grad_copies:
                copy.wait()
            for p in range(parts):
                grads_f[p * toks : (p + 1) * toks, :] = grads[p].astype(F32)
            d_ctx = lax.dot_general(
                grads_f[...].astype(BF16),
                wout_ref[...],
                (((1,), (1,)), ((), ())),
                preferred_element_type=F32,
            )
            for p in range(parts):
                ctx_mine[p] = d_ctx[p * toks : (p + 1) * toks, :].astype(BF16)
            own_ctx.start()
            for copy in ctx_copies:
                copy.start()
            ctx_passes[0].start()
            own_cols.wait()
            for copy in cols_copies:
                copy.wait()
            for copy in cols_shares:
                copy.start()

        return carry

    load(steps - 1).wait()
    lax.fori_loop(0, rounds, body, 0)
    edge.start()

    total = hsum_ref[...]
    high = total.astype(BF16)
    low = (total - high.astype(F32)).astype(BF16)
    resid = jnp.dot(high, wres_ref[...], preferred_element_type=F32)
    resid += jnp.dot(low, wres_ref[...], preferred_element_type=F32)
    pool_ref[st, tm] = ((sums[...] + resid) / POOL).astype(BF16)

    def spread(d):
        return pltpu.make_async_remote_copy(
            src_ref=pool_ref.at[st, tm],
            dst_ref=pool_ref.at[st, tm],
            send_sem=send_pool.at[d],
            recv_sem=recv_pool.at[d],
            device_id=peer_of(lax.rem(mine + d, others)),
            device_id_type=MESH,
        )

    def relay(d):
        flat = lax.rem(mine - d + others, others)
        block = pool_ref.at[lax.rem(flat, chips) * 2 + core, flat // chips]
        return pltpu.make_async_remote_copy(
            src_ref=block,
            dst_ref=block,
            send_sem=send_near.at[d],
            recv_sem=recv_near.at[d],
            device_id={"stream": chip * 2 + 1 - core},
            device_id_type=MESH,
        )

    def launch(d, c):
        spread(d).start()
        return c

    def forward(d, c):
        spread(d).wait_recv()
        relay(d).start()
        return c

    def settle(d, c):
        spread(d).wait_send()
        return c

    def close(d, c):
        relay(d).wait()
        return c

    lax.fori_loop(1, others, launch, 0)
    relay(0).start()
    wt_ref[...] = w_ref[...].T
    fetch.wait()
    wqkvt_ref[...] = wqkv[...].T
    for copy, onward in zip(ctx_copies, ctx_passes[1:]):
        copy.wait_recv()
        onward.start()
    lax.fori_loop(1, others, forward, 0)
    for copy in ctx_copies:
        copy.wait_send()
    for copy in ctx_passes + cols_shares:
        copy.wait()
    own_ctx.wait()
    edge.wait()
    for i in range(steps):
        save(i).wait()

    @pl.when(tm < tms - 1)
    def _():
        halo.wait_send()

    lax.fori_loop(1, others, settle, 0)
    lax.fori_loop(0, others, close, 0)


def front(lengths, signal, w_qkv, w_conv, w_out, w_res, d_out, collective):
    samples, chans = signal.shape
    toks, width = d_out.shape
    tms, parts = lax.axis_size("tm"), lax.axis_size("stream")
    steps = samples // DILATION_STEP
    group = 4
    inner = w_out.shape[0]
    others = tms * parts // 2
    columns = width // tms
    anywhere = pl.BlockSpec(memory_space=pl.ANY)
    dma = pltpu.SemaphoreType.DMA
    return pl.pallas_call(
        functools.partial(front_kernel, steps, group),
        out_shape=[
            jax.ShapeDtypeStruct((samples, 2 * chans), BF16),
            jax.ShapeDtypeStruct((DILATION_STEP, chans), BF16),
            jax.ShapeDtypeStruct((toks, chans), F32),
            jax.ShapeDtypeStruct((parts, tms, toks, chans), BF16),
            jax.ShapeDtypeStruct((tms, parts, toks, inner), BF16),
            jax.ShapeDtypeStruct((parts, tms, toks, columns), BF16),
            jax.ShapeDtypeStruct((parts, 8, 128), jnp.int32),
            jax.ShapeDtypeStruct(w_conv.shape[::-1], BF16),
            jax.ShapeDtypeStruct(w_qkv.shape[::-1], BF16),
        ],
        in_specs=[pl.BlockSpec(memory_space=pltpu.SMEM), anywhere, anywhere] + [VMEM_SPEC] * 4,
        out_specs=[anywhere, anywhere] + [VMEM_SPEC] * 7,
        scratch_shapes=[
            pltpu.VMEM((samples + DILATION_STEP, chans), BF16),
            pltpu.VMEM((samples, 2 * chans), BF16),
            pltpu.VMEM((parts, toks, width), BF16),
            pltpu.VMEM((parts * toks, width), F32),
            pltpu.VMEM(w_qkv.shape, BF16),
            pltpu.VMEM((2 * chans, chans), BF16),
            pltpu.VMEM((parts, toks, inner), BF16),
            pltpu.VMEM((tms, toks, columns), BF16),
            pltpu.VMEM((toks, chans), F32),
            dma((steps,)),
            dma((steps,)),
            dma((3, tms - 1)),
            dma((3, tms - 1)),
            dma((3, parts - 1)),
            dma((3, parts - 1)),
            dma((others,)),
            dma((others,)),
            dma((others,)),
            dma((others,)),
            dma((5,)),
        ],
        compiler_params=pltpu.CompilerParams(collective_id=collective, has_side_effects=True),
        name="front",
    )(lengths, signal, w_qkv, w_conv, w_out, w_res, d_out)


NT = (((1,), (1,)), ((), ()))
TN = (((0,), (0,)), ((), ()))


def fdot(a, b, dims=(((1,), (0,)), ((), ()))):
    return lax.dot_general(a, b, dims, preferred_element_type=F32)


def attend(heads, size, allowed, proj, dctx, ctx, dproj):
    scale = 1.0 / math.sqrt(size)
    span = range(heads)

    def part(h, j):
        base = (3 * h + j) * size
        return proj[:, base : base + size]

    inner = [slice(h * size, (h + 1) * size) for h in span]
    scores = [fdot(part(h, 0), part(h, 1), NT) * scale for h in span]
    d_prob = [fdot(dctx[:, inner[h]], part(h, 2), NT) for h in span]
    scores = [jnp.where(allowed, a, -1e30) for a in scores]
    weights = [jnp.exp(a - jnp.max(a, axis=-1, keepdims=True)) for a in scores]
    prob = [a * (1.0 / jnp.sum(a, axis=-1, keepdims=True)) for a in weights]
    prob16 = [a.astype(BF16) for a in prob]
    d_score = [
        (p * (d - jnp.sum(d * p, axis=-1, keepdims=True))).astype(BF16)
        for p, d in zip(prob, d_prob)
    ]
    for h in span:
        base = 3 * h * size
        ctx[:, inner[h]] = fdot(prob16[h], part(h, 2))
        d_query = scale * fdot(d_score[h], part(h, 1))
        d_key = scale * fdot(d_score[h], part(h, 0), TN)
        d_value = fdot(prob16[h], dctx[:, inner[h]], TN)
        dproj[:, base : base + size] = d_query.astype(BF16)
        dproj[:, base + size : base + 2 * size] = d_key.astype(BF16)
        dproj[:, base + 2 * size : base + 3 * size] = d_value.astype(BF16)


def back_kernel(
    steps, heads, len_ref, lens_ref, sig_hbm, edge_hbm, a_hbm, hsum_ref, pool_ref, ctx_in, cols_in,
    wt_ref, wres_ref, win_ref, wqkv_ref, wqkvt_ref, wout_ref, grad_ref,
    out_ref, dsig_hbm, gconv_ref, gres_ref, gin_ref, gqkv_ref, gout_ref,
    sig, a_buf, dsig, first, arrive, pool_f, pool_b, dctx_f, dctx_b, cols_f, cols_b, tok_v, norm,
    proj, ctx_v, dproj, dg, gin_acc, cols_acc, own_send, own_land, out_send, out_land, cols_mine,
    cols_land, in_parts, in_near, in_sum, in_far, conv_acc, conv_parts, conv_near, conv_sum,
    conv_far, conv_f, conv_rows, conv_rland, conv_own, conv_land, res_acc, res_parts, res_near,
    res_sum, res_far, res_f, res_rows, res_rland, res_own, res_land, dh8, dr8, turned,
    sem_in, sem_a, sem_out, send, recv,
):
    tms, parts = lax.axis_size("tm"), lax.axis_size("stream")
    tm, st = lax.axis_index("tm"), lax.axis_index("stream")
    chips = parts // 2
    core, chip = lax.rem(st, 2), st // 2
    tile = DILATION_STEP
    samples = steps * tile
    chans = wt_ref.shape[1] // 2
    toks, width = grad_ref.shape
    total = tms * toks
    inner = wout_ref.shape[0]
    size = inner // heads
    columns = width // tms
    in_rows = chans // parts

    barrier = pltpu.get_barrier_semaphore()
    for d in range(1, parts):
        pl.semaphore_signal(
            barrier, inc=1, device_id={"stream": lax.rem(st + d, parts)}, device_id_type=MESH
        )
    for d in range(1, tms):
        pl.semaphore_signal(
            barrier, inc=1, device_id={"tm": lax.rem(tm + d, tms)}, device_id_type=MESH
        )

    loads = [pltpu.make_async_copy(edge_hbm, sig.at[pl.ds(0, tile)], sem_in.at[0])]
    loads.append(pltpu.make_async_copy(sig_hbm, sig.at[pl.ds(tile, samples)], sem_in.at[1]))
    loads.append(pltpu.make_async_copy(a_hbm, a_buf, sem_a.at[0]))
    for copy in loads:
        copy.start()

    count = iter(range(send.shape[0]))

    def remote(src, dst, device):
        j = next(count)
        return pltpu.make_async_remote_copy(
            src_ref=src,
            dst_ref=dst,
            send_sem=send.at[j],
            recv_sem=recv.at[j],
            device_id=device,
            device_id_type=MESH,
        )

    def to_stream(d):
        return {"stream": lax.rem(st + d, parts)}

    def to_tm(d):
        return {"tm": lax.rem(tm + d, tms)}

    def to_chip(d):
        return {"stream": lax.rem(chip + d, chips) * 2 + core}

    near = {"stream": chip * 2 + 1 - core}

    def begin(copies):
        for copy in copies:
            copy.start()

    def finish(copies):
        for copy in copies:
            copy.wait()

    row = lax.broadcasted_iota(jnp.int32, (total, total), 0)
    col = lax.broadcasted_iota(jnp.int32, (total, total), 1)
    gout_ref[...] = jnp.zeros_like(gout_ref)
    gqkv_ref[...] = jnp.zeros_like(gqkv_ref)
    gin_acc[...] = jnp.zeros_like(gin_acc)
    cols_acc[...] = jnp.zeros_like(cols_acc)
    mine = pl.ds(pl.multiple_of(tm * toks, 8), toks)

    def stay(s, carry):
        for k in range(tms):
            rows = slice(k * toks, (k + 1) * toks)
            pool_f[rows, :] = pool_ref[s, k].astype(F32)
            dctx_f[rows, :] = ctx_in[k, s].astype(F32)
            cols_f[rows, :] = cols_in[s, k].astype(F32)
        pool_b[...] = pool_f[...].astype(BF16)
        dctx_b[...] = dctx_f[...].astype(BF16)
        cols_b[...] = cols_f[...].astype(BF16)
        tok = fdot(pool_b[...], win_ref[...]).astype(BF16).astype(F32)
        tok_v[...] = tok
        r = lax.rsqrt(jnp.mean(tok * tok, axis=-1, keepdims=True) + EPS)
        norm[...] = (tok * r).astype(BF16)
        proj[...] = fdot(norm[...], wqkv_ref[...]).astype(BF16)
        limit = lens_ref[s, 0:1, 0:1]
        allowed = (col <= row) & (col * POOL < limit)
        attend(heads, size, allowed, proj, dctx_b, ctx_v, dproj)
        context = ctx_v[...].astype(BF16)
        gout_ref[...] += fdot(context, cols_b[...], TN)
        cols_acc[...] += fdot(pool_b[...], cols_b[...], TN)
        if columns % 128 == 0:
            own = norm[:, pl.ds(pl.multiple_of(tm * columns, columns), columns)]
            gqkv_ref[...] += fdot(own, dproj[...], TN)
        else:
            for k in range(tms):

                @pl.when(tm == k)
                def _():
                    own = norm[:, k * columns : (k + 1) * columns]
                    gqkv_ref[...] += fdot(own, dproj[...], TN)

        d_normed = fdot(dproj[...], wqkvt_ref[...])
        tok = tok_v[...]
        along = jnp.sum(d_normed * tok, axis=-1, keepdims=True)
        d_group = r * d_normed - tok * (r * r * r * along / width)
        dg[...] = d_group
        own_send[s] = dg[mine, :].astype(BF16)
        out_send[s] = fdot(ctx_v[mine, :].astype(BF16), wout_ref[...]).astype(BF16)
        gin_acc[...] += fdot(pool_b[...], d_group.astype(BF16), TN)
        return carry

    lax.fori_loop(0, parts, stay, 0)

    own_copies = [
        remote(own_send.at[lax.rem(st + d, parts)], own_land.at[d - 1], to_stream(d))
        for d in range(1, parts)
    ]
    out_copies = [
        remote(out_send.at[lax.rem(st + d, parts)], out_land.at[d - 1], to_stream(d))
        for d in range(1, parts)
    ]
    cols_copies = [remote(cols_mine, cols_land.at[tm], to_tm(d)) for d in range(1, tms)]
    back = remote(first, arrive, {"tm": lax.rem(tm + tms - 1, tms)})

    def reduce_near(blocks, land):
        return [remote(blocks.at[1 - core], land, near)]

    def reduce_far(sums, land):
        return [
            remote(sums.at[lax.rem(chip + d, chips)], land.at[d - 1], to_chip(d))
            for d in range(1, chips)
        ]

    in_one = reduce_near(in_parts, in_near)
    in_two = reduce_far(in_sum, in_far)
    conv_one = reduce_near(conv_parts, conv_near) + reduce_near(res_parts, res_near)
    conv_two = reduce_far(conv_sum, conv_far) + reduce_far(res_sum, res_far)
    conv_three = [
        copy
        for d in range(1, tms)
        for copy in (
            remote(conv_rows.at[lax.rem(tm + d, tms)], conv_rland.at[d - 1], to_tm(d)),
            remote(res_rows.at[lax.rem(tm + d, tms)], res_rland.at[d - 1], to_tm(d)),
        )
    ]
    conv_four = [
        copy
        for d in range(1, tms)
        for copy in (
            remote(conv_own, conv_land.at[tm], to_tm(d)),
            remote(res_own, res_land.at[tm], to_tm(d)),
        )
    ]

    def split(acc, blocks):
        rows = blocks.shape[2]
        for c in range(2):
            for q in range(chips):
                base = (q * 2 + c) * rows
                blocks[c, q] = acc[base : base + rows, :].astype(BF16)

    def add_near(blocks, land, sums):
        for q in range(chips):
            sums[q] = (blocks[core, q].astype(F32) + land[q].astype(F32)).astype(BF16)

    def add_far(sums, land):
        value = sums[chip].astype(F32)
        for d in range(1, chips):
            value += land[d - 1].astype(F32)
        return value

    def cut(value, full, rows):
        full[...] = value
        n = rows.shape[1]
        for k in range(tms):
            rows[k] = full[k * n : (k + 1) * n, :].astype(BF16)

    def add_rows(rows, land, own, gathered):
        value = rows[tm].astype(F32)
        for d in range(1, tms):
            value += land[d - 1].astype(F32)
        own[...] = value.astype(BF16)
        gathered[tm] = value.astype(BF16)

    pl.semaphore_wait(barrier, parts - 1 + tms - 1)
    begin(own_copies)
    split(gin_acc, in_parts)
    cols_mine[...] = cols_acc[pl.ds(pl.multiple_of(st * in_rows, 8), in_rows), :].astype(BF16)
    cols_land[tm] = cols_mine[...]
    begin(in_one)
    begin(out_copies)
    begin(cols_copies)
    own_tok = fdot(pool_ref[st, tm], win_ref[...]).astype(BF16).astype(F32)

    finish(own_copies)
    d_tok = own_send[st].astype(F32) + grad_ref[...].astype(F32)
    for d in range(1, parts):
        d_tok += own_land[d - 1].astype(F32)
    d_pooled = fdot(d_tok.astype(BF16), win_ref[...], NT)
    d_res = (d_pooled / POOL).astype(BF16)
    d_hidden = fdot(d_res, wres_ref[...], NT)
    d_resf = d_res.astype(F32)
    for t in range(toks):
        dh8[t] = jnp.broadcast_to(d_hidden[t : t + 1, :], (8, chans))
        dr8[t] = jnp.broadcast_to(d_resf[t : t + 1, :], (8, chans))
    high = hsum_ref[...].astype(BF16)
    low = (hsum_ref[...] - high.astype(F32)).astype(BF16)
    res_acc[...] = fdot(high, d_res, TN) + fdot(low, d_res, TN)
    split(res_acc, res_parts)

    finish(in_one)
    add_near(in_parts, in_near, in_sum)
    begin(in_two)
    finish(loads)

    per_tile = tile // POOL

    def later_of(i):
        return fdot(a_buf[pl.ds(i * tile, tile), :], wt_ref[:, :chans]).astype(BF16)

    conv_acc[...] = jnp.zeros_like(conv_acc)
    turned[:chans, :] = sig[pl.ds(0, tile), :].T

    def weigh(i, carry):
        rows = pl.ds(i * tile, tile)
        for j in range(per_tile):
            token = i * per_tile + j
            base = pl.ds(token * POOL, POOL)
            gate = dh8[token]
            for c in range(2):
                lanes = slice(c * chans, (c + 1) * chans)
                a = a_buf[base, lanes].astype(F32).reshape(POOL // 8, 8, chans)
                a_buf[base, lanes] = (a * gate[None]).reshape(POOL, chans).astype(BF16)
        dm = a_buf[rows, :]
        turned[chans:, :] = sig[pl.ds((i + 1) * tile, tile), :].T
        conv_acc[...] += fdot(turned[...], dm)
        turned[:chans, :] = turned[chans:, :]

        @pl.when(i == 0)
        def _():
            first[...] = later_of(0)

            @pl.when(tm > 0)
            def _():
                back.start()

        return carry

    lax.fori_loop(0, steps, weigh, 0)

    split(conv_acc, conv_parts)
    begin(conv_one)

    length = len_ref[0]

    def emit(i, later):
        rows = pl.ds(i * tile, tile)
        here = fdot(a_buf[rows, :], wt_ref[:, chans:])
        for j in range(per_tile):
            token = i * per_tile + j
            index = lax.broadcasted_iota(jnp.int32, (POOL, 128), 0) + (tm * samples + token * POOL)
            valid = jnp.where(index < length, 1.0, 0.0)
            valid = jnp.concatenate([valid] * (chans // 128), axis=1)
            own = dr8[token][None] * valid.reshape(POOL // 8, 8, chans)
            part = slice(j * POOL, (j + 1) * POOL)
            value = own.reshape(POOL, chans) + here[part] + later[part].astype(F32)
            dsig[pl.ds(token * POOL, POOL), :] = value.astype(BF16)
        pltpu.make_async_copy(dsig.at[rows], dsig_hbm.at[rows], sem_out.at[i]).start()

    def emit_step(i, carry):
        emit(i, later_of(i + 1))
        return carry

    cuts = [0, steps // 6, steps // 2, steps - 1]
    lax.fori_loop(cuts[0], cuts[1], emit_step, 0)
    finish(conv_one)
    add_near(conv_parts, conv_near, conv_sum)
    add_near(res_parts, res_near, res_sum)
    begin(conv_two)
    lax.fori_loop(cuts[1], cuts[2], emit_step, 0)
    finish(in_two)
    finish(conv_two)
    cut(add_far(conv_sum, conv_far), conv_f, conv_rows)
    cut(add_far(res_sum, res_far), res_f, res_rows)
    begin(conv_three)
    lax.fori_loop(cuts[2], cuts[3], emit_step, 0)

    @pl.when(tm < tms - 1)
    def _():
        back.wait_recv()

    @pl.when(tm == tms - 1)
    def _():
        arrive[...] = jnp.zeros_like(arrive)

    emit(steps - 1, arrive[...])
    finish(out_copies)
    value = own_tok + out_send[st].astype(F32)
    for d in range(1, parts):
        value += out_land[d - 1].astype(F32)
    out_ref[...] = value.astype(BF16)
    finish(cols_copies)
    total_in = add_far(in_sum, in_far)
    for k in range(tms):
        lanes = slice(k * columns, (k + 1) * columns)
        gin_ref[:, lanes] = total_in[:, lanes] + cols_land[k].astype(F32)

    finish(conv_three)
    add_rows(conv_rows, conv_rland, conv_own, conv_land)
    add_rows(res_rows, res_rland, res_own, res_land)
    begin(conv_four)

    @pl.when(tm > 0)
    def _():
        back.wait_send()

    for i in range(steps):
        rows = pl.ds(i * tile, tile)
        pltpu.make_async_copy(dsig.at[rows], dsig_hbm.at[rows], sem_out.at[i]).wait()
    finish(conv_four)
    for k in range(tms):
        n = conv_land.shape[1]
        gconv_ref[k * n : (k + 1) * n, :] = conv_land[k].astype(F32)
        n = res_land.shape[1]
        gres_ref[k * n : (k + 1) * n, :] = res_land[k].astype(F32)


def back(lengths, lens, signal, edge, gates, hsum, pool, ctx, cols, weights, d_out, heads, collective):
    w_convt, w_res, w_in, w_qkv, w_qkvt, w_out = weights
    samples, chans = signal.shape
    toks, width = d_out.shape
    tms, parts = lax.axis_size("tm"), lax.axis_size("stream")
    chips = parts // 2
    steps = samples // DILATION_STEP
    total = toks * tms
    inner = w_out.shape[0]
    triple = w_qkv.shape[1]
    columns = width // tms
    joined = 2 * chans
    conv_n, res_n = joined // parts, chans // parts
    anywhere = pl.BlockSpec(memory_space=pl.ANY)
    dma = pltpu.SemaphoreType.DMA

    def vm(*shape, dtype=BF16):
        return pltpu.VMEM(shape, dtype)

    def reduction(rows, n, lanes):
        return [
            vm(rows, lanes, dtype=F32),
            vm(2, chips, n, lanes),
            vm(chips, n, lanes),
            vm(chips, n, lanes),
            vm(max(chips - 1, 1), n, lanes),
            vm(n, lanes, dtype=F32),
            vm(tms, n // tms, lanes),
            vm(tms - 1, n // tms, lanes),
            vm(n // tms, lanes),
            vm(tms, n // tms, lanes),
        ]

    copies = 2 * (parts - 1) + 5 * (tms - 1) + 1 + 3 + 3 * (chips - 1)
    return pl.pallas_call(
        functools.partial(back_kernel, steps, heads),
        out_shape=[
            jax.ShapeDtypeStruct((toks, width), BF16),
            jax.ShapeDtypeStruct((samples, chans), BF16),
            jax.ShapeDtypeStruct((conv_n, joined), F32),
            jax.ShapeDtypeStruct((res_n, chans), F32),
            jax.ShapeDtypeStruct((res_n, width), F32),
            jax.ShapeDtypeStruct((columns, triple), F32),
            jax.ShapeDtypeStruct((inner, columns), F32),
        ],
        in_specs=[pl.BlockSpec(memory_space=pltpu.SMEM), VMEM_SPEC, anywhere, anywhere, anywhere]
        + [VMEM_SPEC] * 11,
        out_specs=[VMEM_SPEC, anywhere] + [VMEM_SPEC] * 5,
        scratch_shapes=[
            vm(samples + DILATION_STEP, chans),
            vm(samples, joined),
            vm(samples, chans),
            vm(DILATION_STEP, chans),
            vm(DILATION_STEP, chans),
            vm(total, chans, dtype=F32),
            vm(total, chans),
            vm(total, inner, dtype=F32),
            vm(total, inner),
            vm(total, columns, dtype=F32),
            vm(total, columns),
            vm(total, width, dtype=F32),
            vm(total, width),
            vm(total, triple),
            vm(total, inner, dtype=F32),
            vm(total, triple),
            vm(total, width, dtype=F32),
            vm(chans, width, dtype=F32),
            vm(chans, columns, dtype=F32),
            vm(parts, toks, width),
            vm(parts - 1, toks, width),
            vm(parts, toks, width),
            vm(parts - 1, toks, width),
            vm(res_n, columns),
            vm(tms, res_n, columns),
            vm(2, chips, res_n, width),
            vm(chips, res_n, width),
            vm(chips, res_n, width),
            vm(max(chips - 1, 1), res_n, width),
        ]
        + reduction(joined, conv_n, joined)
        + reduction(chans, res_n, chans)
        + [
            vm(toks, 8, chans, dtype=F32),
            vm(toks, 8, chans, dtype=F32),
            vm(joined, DILATION_STEP),
            dma((2,)),
            dma((1,)),
            dma((steps,)),
            dma((copies,)),
            dma((copies,)),
        ],
        compiler_params=pltpu.CompilerParams(
            collective_id=collective, has_side_effects=True, vmem_limit_bytes=60 * 1024 * 1024
        ),
        name="back",
    )(lengths, lens, signal, edge, gates, hsum, pool, ctx, cols, *weights, d_out)


def hand_kernel(cuts, *refs):
    n = len(cuts)
    ins, outs, bufs, (sem_in, sem_out) = refs[:n], refs[n : 2 * n], refs[2 * n : 3 * n], refs[3 * n :]
    pulls, pushes = [], []
    for j, pieces in enumerate(cuts):
        rows = ins[j].shape[0] // pieces
        for k in range(pieces):
            part = pl.ds(k * rows, rows)
            at = len(pulls)
            pulls.append(
                pltpu.make_async_copy(ins[j].at[part], bufs[j].at[part], sem_in.at[at])
            )
            pushes.append(
                pltpu.make_async_copy(bufs[j].at[part], outs[j].at[part], sem_out.at[at])
            )
    for copy in pulls:
        copy.start()
    for pull, push in zip(pulls, pushes):
        pull.wait()
        push.start()
    for copy in pushes:
        copy.wait()


def hand(arrays, cuts):
    anywhere = pl.BlockSpec(memory_space=pl.ANY)
    return pl.pallas_call(
        functools.partial(hand_kernel, cuts),
        out_shape=[jax.ShapeDtypeStruct(a.shape, a.dtype) for a in arrays],
        in_specs=[anywhere] * len(arrays),
        out_specs=[anywhere] * len(arrays),
        scratch_shapes=[pltpu.VMEM(a.shape, a.dtype) for a in arrays]
        + [pltpu.SemaphoreType.DMA((sum(cuts),))] * 2,
        compiler_params=pltpu.CompilerParams(vmem_limit_bytes=60 * 1024 * 1024),
        name="hand",
    )(*arrays)


def local(signal, lengths, w_conv, w_res, w_in, w_qkv, w_out, d_out):
    samples, chans = signal.shape[1:]
    toks, width = d_out.shape[1:]
    flat, grad = signal.reshape(samples, chans), d_out.reshape(toks, width)
    heads = w_out.shape[0] // (width // HEADS)
    gates, edge, hsum, pool, ctx, cols, lens, w_convt, w_qkvt = front(
        lengths, flat, w_qkv, w_conv, w_out, w_res, grad, 0
    )
    weights = (w_convt, w_res, w_in, w_qkv, w_qkvt, w_out)
    results = back(
        lengths, lens, flat, edge, gates, hsum, pool, ctx, cols, weights, grad, heads, 1
    )
    out, d_sig, *grads = hand(results, (1, 12, 1, 1, 1, 1, 1))
    return (out[None], d_sig[None], *grads)


def solution(mesh):
    in_specs = (
        P("stream", "tm", None),
        P("stream"),
        P(),
        P(),
        P(),
        P(None, "stream"),
        P("stream", None),
        P("stream", "tm", None),
    )
    out_specs = (
        P("stream", "tm", None),
        P("stream", "tm", None),
        P("stream", None),
        P("stream", None),
        P("stream", None),
        P("tm", "stream"),
        P("stream", "tm"),
    )
    return jax.shard_map(local, mesh=mesh, in_specs=in_specs, out_specs=out_specs, check_vma=False)
```

```python
import functools
import math

import jax
import jax.numpy as jnp
from jax import lax
from jax.experimental import pallas as pl
from jax.experimental.pallas import tpu as pltpu
from jax.sharding import PartitionSpec as P

HEADS = 16
POOL = 256
DILATION_STEP = 512
EPS = 1e-05
BF16 = jnp.bfloat16
F32 = jnp.float32
MESH = pl.DeviceIdType.MESH
VMEM_SPEC = pl.BlockSpec(memory_space=pltpu.VMEM)


def device_of(tm, stream):
    return {"tm": tm, "stream": stream}


def front_kernel(
    steps, group, len_ref, sig_hbm, wqkv_hbm, w_ref, wout_ref, wres_ref, wgrad_ref,
    a_hbm, edge_hbm, hsum_ref, pool_ref, ctx_ref, cols_ref, lens_ref, wt_ref, wqkvt_ref,
    sig, a_buf, grads, grads_f, wqkv, gate_w, ctx_mine, cols_mine, sums, sem_in, sem_out, send_tm, recv_tm,
    send_st, recv_st, send_pool, recv_pool, send_near, recv_near, keep,
):
    tms, parts = lax.axis_size("tm"), lax.axis_size("stream")
    tm, st = lax.axis_index("tm"), lax.axis_index("stream")
    chips = parts // 2
    core, chip = lax.rem(st, 2), st // 2
    mine = tm * chips + chip
    tile = DILATION_STEP
    samples = steps * tile
    chans = w_ref.shape[1] // 2
    toks = samples // POOL
    rounds = steps // group

    def peer_of(flat):
        return device_of(flat // chips, lax.rem(flat, chips) * 2 + core)

    barrier = pltpu.get_barrier_semaphore()

    def greet(device):
        pl.semaphore_signal(barrier, inc=1, device_id=device, device_id_type=MESH)

    others = tms * chips
    lax.fori_loop(1, others, lambda d, c: (greet(peer_of(lax.rem(mine + d, others))), c)[1], 0)
    for d in range(chips):
        greet(device_of(tm, lax.rem(chip + d, chips) * 2 + 1 - core))

    def load(i):
        return pltpu.make_async_copy(
            sig_hbm.at[pl.ds(i * tile, tile)], sig.at[pl.ds((i + 1) * tile, tile)], sem_in.at[i]
        )

    def save(i):
        return pltpu.make_async_copy(
            a_buf.at[pl.ds(i * tile, tile)], a_hbm.at[pl.ds(i * tile, tile)], sem_out.at[i]
        )

    for i in reversed(range(steps)):
        load(i).start()
    fetch = pltpu.make_async_copy(wqkv_hbm, wqkv, keep.at[4])
    fetch.start()
    gate_w[...] = w_ref[:, chans:] * jnp.asarray(0.5, BF16)

    halo = pltpu.make_async_remote_copy(
        src_ref=sig_hbm.at[pl.ds(samples - tile, tile)],
        dst_ref=sig.at[pl.ds(0, tile)],
        send_sem=send_tm.at[2, 0],
        recv_sem=recv_tm.at[2, 0],
        device_id={"tm": lax.rem(tm + 1, tms)},
        device_id_type=MESH,
    )

    def to_stream(j, d, src, dst):
        return pltpu.make_async_remote_copy(
            src_ref=src,
            dst_ref=dst,
            send_sem=send_st.at[j, d - 1],
            recv_sem=recv_st.at[j, d - 1],
            device_id={"stream": lax.rem(st + d, parts)},
            device_id_type=MESH,
        )

    grad_copies = [
        copy
        for d in range(1, parts)
        for copy in (
            to_stream(0, d, wgrad_ref, grads.at[st]),
            to_stream(1, d, lens_ref.at[st], lens_ref.at[st]),
        )
    ]

    def to_tm(j, d, src, dst, device):
        return pltpu.make_async_remote_copy(
            src_ref=src,
            dst_ref=dst,
            send_sem=send_tm.at[j, d - 1],
            recv_sem=recv_tm.at[j, d - 1],
            device_id=device,
            device_id_type=MESH,
        )

    width = grads.shape[2]
    columns = width // tms

    pairs = tms // 2
    across = {"tm": tm + 1 - 2 * lax.rem(tm, 2)}
    ctx_copies = [
        to_tm(0, d, ctx_mine, ctx_ref.at[tm], {"tm": lax.rem(tm + 2 * d, tms)})
        for d in range(1, pairs)
    ]
    ctx_passes = []
    for d in range(pairs):
        block = ctx_ref.at[lax.rem(tm - 2 * d + tms, tms)]
        ctx_passes.append(to_tm(0, pairs + d, block if d else ctx_mine, block, across))
    cols_copies = [
        to_tm(
            1, d, cols_mine.at[lax.rem(tm + d, tms)], cols_ref.at[st, tm],
            {"tm": lax.rem(tm + d, tms)},
        )
        for d in range(1, tms)
    ]
    cols_shares = [to_stream(2, d, cols_ref.at[st], cols_ref.at[st]) for d in range(1, parts)]
    own_grad = pltpu.make_async_copy(wgrad_ref, grads.at[st], keep.at[0])
    own_ctx = pltpu.make_async_copy(ctx_mine, ctx_ref.at[tm], keep.at[1])
    own_cols = pltpu.make_async_copy(cols_mine.at[tm], cols_ref.at[st, tm], keep.at[2])
    edge = pltpu.make_async_copy(sig.at[pl.ds(0, tile)], edge_hbm, keep.at[3])

    for k in range(tms):
        cols_mine[k] = wgrad_ref[:, k * columns : (k + 1) * columns]
    lens_ref[st] = jnp.full(lens_ref.shape[1:], len_ref[0], jnp.int32)
    length = len_ref[0]

    def chunk(token):
        base = token * POOL
        past = sig[pl.ds(base, POOL), :]
        cur = sig[pl.ds(base + tile, POOL), :]
        mixed_f = jnp.dot(past, w_ref[:chans, :chans], preferred_element_type=F32)
        mixed_f += jnp.dot(cur, w_ref[chans:, :chans], preferred_element_type=F32)
        mixed_g = jnp.dot(past, gate_w[:chans], preferred_element_type=F32)
        mixed_g += jnp.dot(cur, gate_w[chans:], preferred_element_type=F32)
        row = lax.broadcasted_iota(jnp.int32, (POOL, 128), 0) + (tm * samples + base)
        half = jnp.where(row < length, 0.5, 0.0)
        half = jnp.concatenate([half] * (chans // 128), axis=1)
        t = jnp.tanh(mixed_f)
        s = half * jnp.tanh(mixed_g) + half
        h = t * s
        a_buf[pl.ds(base, POOL), :chans] = (s - t * h).astype(BF16)
        a_buf[pl.ds(base, POOL), chans:] = (h - h * s).astype(BF16)
        hs = jnp.sum(h, axis=0, keepdims=True)
        ss = jnp.sum(cur.astype(F32) * half, axis=0, keepdims=True) * 2.0
        return hs, ss

    def body(it, carry):
        r = rounds - 1 - it
        per_tile = tile // POOL
        rows = [None] * (group * per_tile)
        for k in reversed(range(group)):
            i = r * group + k
            if k > 0:
                load(i - 1).wait()
            else:

                @pl.when(r > 0)
                def _():
                    load(i - 1).wait()

                @pl.when((r == 0) & (tm > 0))
                def _():
                    halo.wait_recv()

                @pl.when((r == 0) & (tm == 0))
                def _():
                    sig[pl.ds(0, tile), :] = jnp.zeros((tile, chans), BF16)

            for j in range(per_tile):
                rows[k * per_tile + j] = chunk(i * per_tile + j)
            save(i).start()
        block = pl.ds(pl.multiple_of(r * group * per_tile, 8), group * per_tile)
        hsum_ref[block, :] = jnp.concatenate([a for a, _ in rows], axis=0)
        sums[block, :] = jnp.concatenate([b for _, b in rows], axis=0)

        @pl.when(it == 1)
        def _():
            own_grad.wait()
            for copy in grad_copies:
                copy.wait()
            for p in range(parts):
                grads_f[p * toks : (p + 1) * toks, :] = grads[p].astype(F32)
            d_ctx = lax.dot_general(
                grads_f[...].astype(BF16),
                wout_ref[...],
                (((1,), (1,)), ((), ())),
                preferred_element_type=F32,
            )
            for p in range(parts):
                ctx_mine[p] = d_ctx[p * toks : (p + 1) * toks, :].astype(BF16)
            own_ctx.start()
            for copy in ctx_copies:
                copy.start()
            ctx_passes[0].start()
            own_cols.wait()
            for copy in cols_copies:
                copy.wait()
            for copy in cols_shares:
                copy.start()

        return carry

    pl.semaphore_wait(barrier, others - 1 + chips)

    @pl.when(tm < tms - 1)
    def _():
        halo.start()

    own_grad.start()
    own_cols.start()
    for copy in grad_copies + cols_copies:
        copy.start()
    load(steps - 1).wait()
    lax.fori_loop(0, rounds, body, 0)
    edge.start()

    total = hsum_ref[...]
    high = total.astype(BF16)
    low = (total - high.astype(F32)).astype(BF16)
    resid = jnp.dot(high, wres_ref[...], preferred_element_type=F32)
    resid += jnp.dot(low, wres_ref[...], preferred_element_type=F32)
    pool_ref[st, tm] = ((sums[...] + resid) / POOL).astype(BF16)

    def spread(d):
        return pltpu.make_async_remote_copy(
            src_ref=pool_ref.at[st, tm],
            dst_ref=pool_ref.at[st, tm],
            send_sem=send_pool.at[d],
            recv_sem=recv_pool.at[d],
            device_id=peer_of(lax.rem(mine + d, others)),
            device_id_type=MESH,
        )

    def relay(d):
        flat = lax.rem(mine - d + others, others)
        block = pool_ref.at[lax.rem(flat, chips) * 2 + core, flat // chips]
        return pltpu.make_async_remote_copy(
            src_ref=block,
            dst_ref=block,
            send_sem=send_near.at[d],
            recv_sem=recv_near.at[d],
            device_id={"stream": chip * 2 + 1 - core},
            device_id_type=MESH,
        )

    def launch(d, c):
        spread(d).start()
        return c

    def forward(d, c):
        spread(d).wait_recv()
        relay(d).start()
        return c

    def settle(d, c):
        spread(d).wait_send()
        return c

    def close(d, c):
        relay(d).wait()
        return c

    lax.fori_loop(1, others, launch, 0)
    relay(0).start()
    wt_ref[...] = w_ref[...].T
    fetch.wait()
    wqkvt_ref[...] = wqkv[...].T
    for copy, onward in zip(ctx_copies, ctx_passes[1:]):
        copy.wait_recv()
        onward.start()
    lax.fori_loop(1, others, forward, 0)
    for copy in ctx_copies:
        copy.wait_send()
    for copy in ctx_passes + cols_shares:
        copy.wait()
    own_ctx.wait()
    edge.wait()
    for i in range(steps):
        save(i).wait()

    @pl.when(tm < tms - 1)
    def _():
        halo.wait_send()

    lax.fori_loop(1, others, settle, 0)
    lax.fori_loop(0, others, close, 0)


def front(lengths, signal, w_qkv, w_conv, w_out, w_res, d_out, collective):
    samples, chans = signal.shape
    toks, width = d_out.shape
    tms, parts = lax.axis_size("tm"), lax.axis_size("stream")
    steps = samples // DILATION_STEP
    group = 4
    inner = w_out.shape[0]
    others = tms * parts // 2
    columns = width // tms
    anywhere = pl.BlockSpec(memory_space=pl.ANY)
    dma = pltpu.SemaphoreType.DMA
    return pl.pallas_call(
        functools.partial(front_kernel, steps, group),
        out_shape=[
            jax.ShapeDtypeStruct((samples, 2 * chans), BF16),
            jax.ShapeDtypeStruct((DILATION_STEP, chans), BF16),
            jax.ShapeDtypeStruct((toks, chans), F32),
            jax.ShapeDtypeStruct((parts, tms, toks, chans), BF16),
            jax.ShapeDtypeStruct((tms, parts, toks, inner), BF16),
            jax.ShapeDtypeStruct((parts, tms, toks, columns), BF16),
            jax.ShapeDtypeStruct((parts, 8, 128), jnp.int32),
            jax.ShapeDtypeStruct(w_conv.shape[::-1], BF16),
            jax.ShapeDtypeStruct(w_qkv.shape[::-1], BF16),
        ],
        in_specs=[pl.BlockSpec(memory_space=pltpu.SMEM), anywhere, anywhere] + [VMEM_SPEC] * 4,
        out_specs=[anywhere, anywhere] + [VMEM_SPEC] * 7,
        scratch_shapes=[
            pltpu.VMEM((samples + DILATION_STEP, chans), BF16),
            pltpu.VMEM((samples, 2 * chans), BF16),
            pltpu.VMEM((parts, toks, width), BF16),
            pltpu.VMEM((parts * toks, width), F32),
            pltpu.VMEM(w_qkv.shape, BF16),
            pltpu.VMEM((2 * chans, chans), BF16),
            pltpu.VMEM((parts, toks, inner), BF16),
            pltpu.VMEM((tms, toks, columns), BF16),
            pltpu.VMEM((toks, chans), F32),
            dma((steps,)),
            dma((steps,)),
            dma((3, tms - 1)),
            dma((3, tms - 1)),
            dma((3, parts - 1)),
            dma((3, parts - 1)),
            dma((others,)),
            dma((others,)),
            dma((others,)),
            dma((others,)),
            dma((5,)),
        ],
        compiler_params=pltpu.CompilerParams(collective_id=collective, has_side_effects=True),
        name="front",
    )(lengths, signal, w_qkv, w_conv, w_out, w_res, d_out)


NT = (((1,), (1,)), ((), ()))
TN = (((0,), (0,)), ((), ()))


def fdot(a, b, dims=(((1,), (0,)), ((), ()))):
    return lax.dot_general(a, b, dims, preferred_element_type=F32)


def attend(heads, size, allowed, proj, dctx, ctx, dproj):
    scale = 1.0 / math.sqrt(size)
    span = range(heads)

    def part(h, j):
        base = (3 * h + j) * size
        return proj[:, base : base + size]

    inner = [slice(h * size, (h + 1) * size) for h in span]
    scores = [fdot(part(h, 0), part(h, 1), NT) * scale for h in span]
    d_prob = [fdot(dctx[:, inner[h]], part(h, 2), NT) for h in span]
    scores = [jnp.where(allowed, a, -1e30) for a in scores]
    weights = [jnp.exp(a - jnp.max(a, axis=-1, keepdims=True)) for a in scores]
    prob = [a * (1.0 / jnp.sum(a, axis=-1, keepdims=True)) for a in weights]
    prob16 = [a.astype(BF16) for a in prob]
    d_score = [
        (p * (d - jnp.sum(d * p, axis=-1, keepdims=True))).astype(BF16)
        for p, d in zip(prob, d_prob)
    ]
    for h in span:
        base = 3 * h * size
        ctx[:, inner[h]] = fdot(prob16[h], part(h, 2))
        d_query = scale * fdot(d_score[h], part(h, 1))
        d_key = scale * fdot(d_score[h], part(h, 0), TN)
        d_value = fdot(prob16[h], dctx[:, inner[h]], TN)
        dproj[:, base : base + size] = d_query.astype(BF16)
        dproj[:, base + size : base + 2 * size] = d_key.astype(BF16)
        dproj[:, base + 2 * size : base + 3 * size] = d_value.astype(BF16)


def back_kernel(
    steps, heads, len_ref, lens_ref, sig_hbm, edge_hbm, a_hbm, hsum_ref, pool_ref, ctx_in, cols_in,
    wt_ref, wres_ref, win_ref, wqkv_ref, wqkvt_ref, wout_ref, grad_ref,
    out_ref, dsig_hbm, gconv_ref, gres_ref, gin_ref, gqkv_ref, gout_ref,
    sig, a_buf, dsig, first, arrive, pool_f, pool_b, dctx_f, dctx_b, cols_f, cols_b, tok_v, norm,
    proj, ctx_v, dproj, dg, gin_acc, cols_acc, own_send, own_land, out_send, out_land, cols_mine,
    cols_land, in_parts, in_near, in_sum, in_far, conv_acc, conv_parts, conv_near, conv_sum,
    conv_far, conv_f, conv_rows, conv_rland, conv_own, conv_land, res_acc, res_parts, res_near,
    res_sum, res_far, res_f, res_rows, res_rland, res_own, res_land, dh8, dr8, turned, rate,
    sem_in, sem_a, sem_out, send, recv,
):
    tms, parts = lax.axis_size("tm"), lax.axis_size("stream")
    tm, st = lax.axis_index("tm"), lax.axis_index("stream")
    chips = parts // 2
    core, chip = lax.rem(st, 2), st // 2
    tile = DILATION_STEP
    samples = steps * tile
    chans = wt_ref.shape[1] // 2
    toks, width = grad_ref.shape
    total = tms * toks
    inner = wout_ref.shape[0]
    size = inner // heads
    columns = width // tms
    in_rows = chans // parts

    barrier = pltpu.get_barrier_semaphore()
    for d in range(1, parts):
        pl.semaphore_signal(
            barrier, inc=1, device_id={"stream": lax.rem(st + d, parts)}, device_id_type=MESH
        )
    for d in range(1, tms):
        pl.semaphore_signal(
            barrier, inc=1, device_id={"tm": lax.rem(tm + d, tms)}, device_id_type=MESH
        )

    loads = [pltpu.make_async_copy(edge_hbm, sig.at[pl.ds(0, tile)], sem_in.at[0])]
    loads.append(pltpu.make_async_copy(sig_hbm, sig.at[pl.ds(tile, samples)], sem_in.at[1]))
    loads.append(pltpu.make_async_copy(a_hbm, a_buf, sem_a.at[0]))
    for copy in loads:
        copy.start()

    count = iter(range(send.shape[0]))

    def remote(src, dst, device):
        j = next(count)
        return pltpu.make_async_remote_copy(
            src_ref=src,
            dst_ref=dst,
            send_sem=send.at[j],
            recv_sem=recv.at[j],
            device_id=device,
            device_id_type=MESH,
        )

    def to_stream(d):
        return {"stream": lax.rem(st + d, parts)}

    def to_tm(d):
        return {"tm": lax.rem(tm + d, tms)}

    def to_chip(d):
        return {"stream": lax.rem(chip + d, chips) * 2 + core}

    near = {"stream": chip * 2 + 1 - core}

    def begin(copies):
        for copy in copies:
            copy.start()

    def finish(copies):
        for copy in copies:
            copy.wait()

    row = lax.broadcasted_iota(jnp.int32, (total, total), 0)
    col = lax.broadcasted_iota(jnp.int32, (total, total), 1)
    gout_ref[...] = jnp.zeros_like(gout_ref)
    gqkv_ref[...] = jnp.zeros_like(gqkv_ref)
    gin_acc[...] = jnp.zeros_like(gin_acc)
    cols_acc[...] = jnp.zeros_like(cols_acc)
    batch = pool_b.shape[0] // total

    def lead(b):
        for s in range(batch):
            for k in range(tms):
                rows = slice(s * total + k * toks, s * total + (k + 1) * toks)
                pool_f[rows, :] = pool_ref[b * batch + s, k].astype(F32)
                dctx_f[rows, :] = ctx_in[k, b * batch + s].astype(F32)
                cols_f[rows, :] = cols_in[b * batch + s, k].astype(F32)
        pool_b[...] = pool_f[...].astype(BF16)
        dctx_b[...] = dctx_f[...].astype(BF16)
        cols_b[...] = cols_f[...].astype(BF16)
        tok_v[...] = fdot(pool_b[...], win_ref[...]).astype(BF16).astype(F32)

        def scaled(s, c):
            rows = pl.ds(pl.multiple_of(s * total, total), total)
            tok = tok_v[rows, :]
            r = lax.rsqrt(jnp.mean(tok * tok, axis=-1, keepdims=True) + EPS)
            norm[rows, :] = (tok * r).astype(BF16)
            rate[rows, :] = jnp.broadcast_to(r, (total, 128))
            return c

        lax.fori_loop(0, batch, scaled, 0)
        proj[...] = fdot(norm[...], wqkv_ref[...]).astype(BF16)

        def look(s, c):
            rows = pl.ds(pl.multiple_of(s * total, total), total)
            limit = lens_ref[b * batch + s, 0:1, 0:1]
            allowed = (col <= row) & (col * POOL < limit)
            attend(
                heads, size, allowed, proj.at[rows], dctx_b.at[rows], ctx_v.at[rows], dproj.at[rows]
            )
            return c

        lax.fori_loop(0, batch, look, 0)
        dg[...] = fdot(dproj[...], wqkvt_ref[...])

        def through(s, c):
            rows = pl.ds(pl.multiple_of(s * total, total), total)
            own = pl.ds(pl.multiple_of(s * total + tm * toks, 8), toks)
            d_normed, tok = dg[rows, :], tok_v[rows, :]
            r = rate[rows, 0:1]
            along = jnp.sum(d_normed * tok, axis=-1, keepdims=True)
            dg[rows, :] = r * d_normed - tok * (r * r * r * along / width)
            own_send[b * batch + s] = dg[own, :].astype(BF16)
            return c

        lax.fori_loop(0, batch, through, 0)

    def follow(b):
        for s in range(batch):
            own = pl.ds(pl.multiple_of(s * total + tm * toks, 8), toks)
            value = fdot(ctx_v[own, :].astype(BF16), wout_ref[...])
            out_send[b * batch + s] = value.astype(BF16)
        gin_acc[...] += fdot(pool_b[...], dg[...].astype(BF16), TN)
        cols_acc[...] += fdot(pool_b[...], cols_b[...], TN)

    def weights(b):
        gout_ref[...] += fdot(ctx_v[...].astype(BF16), cols_b[...], TN)
        if columns % 128 == 0:
            own = norm[:, pl.ds(pl.multiple_of(tm * columns, columns), columns)]
            gqkv_ref[...] += fdot(own, dproj[...], TN)
        else:
            for k in range(tms):

                @pl.when(tm == k)
                def _():
                    own = norm[:, k * columns : (k + 1) * columns]
                    gqkv_ref[...] += fdot(own, dproj[...], TN)

    batches = parts // batch

    def whole_batch(b, c):
        lead(b)
        follow(b)
        weights(b)
        return c

    if batches > 1:
        lax.fori_loop(0, batches - 1, whole_batch, 0)
    lead(batches - 1)

    own_copies = [
        remote(own_send.at[lax.rem(st + d, parts)], own_land.at[d - 1], to_stream(d))
        for d in range(1, parts)
    ]
    out_copies = [
        remote(out_send.at[lax.rem(st + d, parts)], out_land.at[d - 1], to_stream(d))
        for d in range(1, parts)
    ]
    cols_copies = [remote(cols_mine, cols_land.at[tm], to_tm(d)) for d in range(1, tms)]
    back = remote(first, arrive, {"tm": lax.rem(tm + tms - 1, tms)})

    def reduce_near(blocks, land):
        return [remote(blocks.at[1 - core], land, near)]

    def reduce_far(sums, land):
        return [
            remote(sums.at[lax.rem(chip + d, chips)], land.at[d - 1], to_chip(d))
            for d in range(1, chips)
        ]

    in_one = reduce_near(in_parts, in_near)
    in_two = reduce_far(in_sum, in_far)
    conv_one = reduce_near(conv_parts, conv_near) + reduce_near(res_parts, res_near)
    conv_two = reduce_far(conv_sum, conv_far) + reduce_far(res_sum, res_far)
    conv_three = [
        copy
        for d in range(1, tms)
        for copy in (
            remote(conv_rows.at[lax.rem(tm + d, tms)], conv_rland.at[d - 1], to_tm(d)),
            remote(res_rows.at[lax.rem(tm + d, tms)], res_rland.at[d - 1], to_tm(d)),
        )
    ]
    conv_four = [
        copy
        for d in range(1, tms)
        for copy in (
            remote(conv_own, conv_land.at[tm], to_tm(d)),
            remote(res_own, res_land.at[tm], to_tm(d)),
        )
    ]

    def split(acc, blocks):
        rows = blocks.shape[2]
        for c in range(2):
            for q in range(chips):
                base = (q * 2 + c) * rows
                blocks[c, q] = acc[base : base + rows, :].astype(BF16)

    def add_near(blocks, land, sums):
        for q in range(chips):
            sums[q] = (blocks[core, q].astype(F32) + land[q].astype(F32)).astype(BF16)

    def add_far(sums, land):
        value = sums[chip].astype(F32)
        for d in range(1, chips):
            value += land[d - 1].astype(F32)
        return value

    def cut(value, full, rows):
        full[...] = value
        n = rows.shape[1]
        for k in range(tms):
            rows[k] = full[k * n : (k + 1) * n, :].astype(BF16)

    def add_rows(rows, land, own, gathered):
        value = rows[tm].astype(F32)
        for d in range(1, tms):
            value += land[d - 1].astype(F32)
        own[...] = value.astype(BF16)
        gathered[tm] = value.astype(BF16)

    pl.semaphore_wait(barrier, parts - 1 + tms - 1)
    begin(own_copies)
    follow(batches - 1)
    split(gin_acc, in_parts)
    cols_mine[...] = cols_acc[pl.ds(pl.multiple_of(st * in_rows, 8), in_rows), :].astype(BF16)
    cols_land[tm] = cols_mine[...]
    begin(in_one)
    begin(out_copies)
    begin(cols_copies)
    own_tok = fdot(pool_ref[st, tm], win_ref[...]).astype(BF16).astype(F32)

    finish(own_copies)
    d_tok = own_send[st].astype(F32) + grad_ref[...].astype(F32)
    for d in range(1, parts):
        d_tok += own_land[d - 1].astype(F32)
    d_pooled = fdot(d_tok.astype(BF16), win_ref[...], NT)
    d_res = (d_pooled / POOL).astype(BF16)
    d_hidden = fdot(d_res, wres_ref[...], NT)
    d_resf = d_res.astype(F32)
    for t in range(toks):
        dh8[t] = jnp.broadcast_to(d_hidden[t : t + 1, :], (8, chans))
        dr8[t] = jnp.broadcast_to(d_resf[t : t + 1, :], (8, chans))
    high = hsum_ref[...].astype(BF16)
    low = (hsum_ref[...] - high.astype(F32)).astype(BF16)
    res_acc[...] = fdot(high, d_res, TN) + fdot(low, d_res, TN)
    split(res_acc, res_parts)

    finish(in_one)
    add_near(in_parts, in_near, in_sum)
    begin(in_two)
    finish(loads)

    per_tile = tile // POOL

    def later_of(i):
        return fdot(a_buf[pl.ds(i * tile, tile), :], wt_ref[:, :chans]).astype(BF16)

    conv_acc[...] = jnp.zeros_like(conv_acc)
    turned[:chans, :] = sig[pl.ds(0, tile), :].T

    def weigh(i, carry):
        rows = pl.ds(i * tile, tile)
        for j in range(per_tile):
            token = i * per_tile + j
            base = pl.ds(token * POOL, POOL)
            gate = dh8[token]
            for c in range(2):
                lanes = slice(c * chans, (c + 1) * chans)
                a = a_buf[base, lanes].astype(F32).reshape(POOL // 8, 8, chans)
                a_buf[base, lanes] = (a * gate[None]).reshape(POOL, chans).astype(BF16)
        dm = a_buf[rows, :]
        turned[chans:, :] = sig[pl.ds((i + 1) * tile, tile), :].T
        conv_acc[...] += fdot(turned[...], dm)
        turned[:chans, :] = turned[chans:, :]

        @pl.when(i == 0)
        def _():
            first[...] = later_of(0)

            @pl.when(tm > 0)
            def _():
                back.start()

        return carry

    lax.fori_loop(0, steps, weigh, 0)

    split(conv_acc, conv_parts)
    begin(conv_one)
    weights(batches - 1)

    length = len_ref[0]

    def emit(i, later):
        rows = pl.ds(i * tile, tile)
        here = fdot(a_buf[rows, :], wt_ref[:, chans:])
        for j in range(per_tile):
            token = i * per_tile + j
            index = lax.broadcasted_iota(jnp.int32, (POOL, 128), 0) + (tm * samples + token * POOL)
            valid = jnp.where(index < length, 1.0, 0.0)
            valid = jnp.concatenate([valid] * (chans // 128), axis=1)
            own = dr8[token][None] * valid.reshape(POOL // 8, 8, chans)
            part = slice(j * POOL, (j + 1) * POOL)
            value = own.reshape(POOL, chans) + here[part] + later[part].astype(F32)
            dsig[pl.ds(token * POOL, POOL), :] = value.astype(BF16)
        pltpu.make_async_copy(dsig.at[rows], dsig_hbm.at[rows], sem_out.at[i]).start()

    def emit_step(i, carry):
        emit(i, later_of(i + 1))
        return carry

    cuts = [0, steps // 6, steps // 2, steps - 1]
    lax.fori_loop(cuts[0], cuts[1], emit_step, 0)
    finish(conv_one)
    add_near(conv_parts, conv_near, conv_sum)
    add_near(res_parts, res_near, res_sum)
    begin(conv_two)
    lax.fori_loop(cuts[1], cuts[2], emit_step, 0)
    finish(in_two)
    finish(conv_two)
    cut(add_far(conv_sum, conv_far), conv_f, conv_rows)
    cut(add_far(res_sum, res_far), res_f, res_rows)
    begin(conv_three)
    lax.fori_loop(cuts[2], cuts[3], emit_step, 0)

    @pl.when(tm < tms - 1)
    def _():
        back.wait_recv()

    @pl.when(tm == tms - 1)
    def _():
        arrive[...] = jnp.zeros_like(arrive)

    emit(steps - 1, arrive[...])
    finish(out_copies)
    value = own_tok + out_send[st].astype(F32)
    for d in range(1, parts):
        value += out_land[d - 1].astype(F32)
    out_ref[...] = value.astype(BF16)
    finish(cols_copies)
    total_in = add_far(in_sum, in_far)
    for k in range(tms):
        lanes = slice(k * columns, (k + 1) * columns)
        gin_ref[:, lanes] = total_in[:, lanes] + cols_land[k].astype(F32)

    finish(conv_three)
    add_rows(conv_rows, conv_rland, conv_own, conv_land)
    add_rows(res_rows, res_rland, res_own, res_land)
    begin(conv_four)

    @pl.when(tm > 0)
    def _():
        back.wait_send()

    for i in range(steps):
        rows = pl.ds(i * tile, tile)
        pltpu.make_async_copy(dsig.at[rows], dsig_hbm.at[rows], sem_out.at[i]).wait()
    finish(conv_four)
    for k in range(tms):
        n = conv_land.shape[1]
        gconv_ref[k * n : (k + 1) * n, :] = conv_land[k].astype(F32)
        n = res_land.shape[1]
        gres_ref[k * n : (k + 1) * n, :] = res_land[k].astype(F32)


def back(lengths, lens, signal, edge, gates, hsum, pool, ctx, cols, weights, d_out, heads, collective):
    w_convt, w_res, w_in, w_qkv, w_qkvt, w_out = weights
    samples, chans = signal.shape
    toks, width = d_out.shape
    tms, parts = lax.axis_size("tm"), lax.axis_size("stream")
    chips = parts // 2
    steps = samples // DILATION_STEP
    total = toks * tms
    rows = total * max(n for n in range(1, parts + 1) if parts % n == 0 and (n == 1 or n * total <= 768))
    inner = w_out.shape[0]
    triple = w_qkv.shape[1]
    columns = width // tms
    joined = 2 * chans
    conv_n, res_n = joined // parts, chans // parts
    anywhere = pl.BlockSpec(memory_space=pl.ANY)
    dma = pltpu.SemaphoreType.DMA

    def vm(*shape, dtype=BF16):
        return pltpu.VMEM(shape, dtype)

    def reduction(size, n, lanes):
        return [
            vm(size, lanes, dtype=F32),
            vm(2, chips, n, lanes),
            vm(chips, n, lanes),
            vm(chips, n, lanes),
            vm(max(chips - 1, 1), n, lanes),
            vm(n, lanes, dtype=F32),
            vm(tms, n // tms, lanes),
            vm(tms - 1, n // tms, lanes),
            vm(n // tms, lanes),
            vm(tms, n // tms, lanes),
        ]

    copies = 2 * (parts - 1) + 5 * (tms - 1) + 1 + 3 + 3 * (chips - 1)
    return pl.pallas_call(
        functools.partial(back_kernel, steps, heads),
        out_shape=[
            jax.ShapeDtypeStruct((toks, width), BF16),
            jax.ShapeDtypeStruct((samples, chans), BF16),
            jax.ShapeDtypeStruct((conv_n, joined), F32),
            jax.ShapeDtypeStruct((res_n, chans), F32),
            jax.ShapeDtypeStruct((res_n, width), F32),
            jax.ShapeDtypeStruct((columns, triple), F32),
            jax.ShapeDtypeStruct((inner, columns), F32),
        ],
        in_specs=[pl.BlockSpec(memory_space=pltpu.SMEM), VMEM_SPEC, anywhere, anywhere, anywhere]
        + [VMEM_SPEC] * 11,
        out_specs=[VMEM_SPEC, anywhere] + [VMEM_SPEC] * 5,
        scratch_shapes=[
            vm(samples + DILATION_STEP, chans),
            vm(samples, joined),
            vm(samples, chans),
            vm(DILATION_STEP, chans),
            vm(DILATION_STEP, chans),
            vm(rows, chans, dtype=F32),
            vm(rows, chans),
            vm(rows, inner, dtype=F32),
            vm(rows, inner),
            vm(rows, columns, dtype=F32),
            vm(rows, columns),
            vm(rows, width, dtype=F32),
            vm(rows, width),
            vm(rows, triple),
            vm(rows, inner, dtype=F32),
            vm(rows, triple),
            vm(rows, width, dtype=F32),
            vm(chans, width, dtype=F32),
            vm(chans, columns, dtype=F32),
            vm(parts, toks, width),
            vm(parts - 1, toks, width),
            vm(parts, toks, width),
            vm(parts - 1, toks, width),
            vm(res_n, columns),
            vm(tms, res_n, columns),
            vm(2, chips, res_n, width),
            vm(chips, res_n, width),
            vm(chips, res_n, width),
            vm(max(chips - 1, 1), res_n, width),
        ]
        + reduction(joined, conv_n, joined)
        + reduction(chans, res_n, chans)
        + [
            vm(toks, 8, chans, dtype=F32),
            vm(toks, 8, chans, dtype=F32),
            vm(joined, DILATION_STEP),
            vm(rows, 128, dtype=F32),
            dma((2,)),
            dma((1,)),
            dma((steps,)),
            dma((copies,)),
            dma((copies,)),
        ],
        compiler_params=pltpu.CompilerParams(
            collective_id=collective, has_side_effects=True, vmem_limit_bytes=60 * 1024 * 1024
        ),
        name="back",
    )(lengths, lens, signal, edge, gates, hsum, pool, ctx, cols, *weights, d_out)


def hand_kernel(cuts, *refs):
    n = len(cuts)
    ins, outs, bufs, (sem_in, sem_out) = refs[:n], refs[n : 2 * n], refs[2 * n : 3 * n], refs[3 * n :]
    pulls, pushes = [], []
    for j, pieces in enumerate(cuts):
        rows = ins[j].shape[0] // pieces
        for k in range(pieces):
            part = pl.ds(k * rows, rows)
            at = len(pulls)
            pulls.append(
                pltpu.make_async_copy(ins[j].at[part], bufs[j].at[part], sem_in.at[at])
            )
            pushes.append(
                pltpu.make_async_copy(bufs[j].at[part], outs[j].at[part], sem_out.at[at])
            )
    for copy in pulls:
        copy.start()
    for pull, push in zip(pulls, pushes):
        pull.wait()
        push.start()
    for copy in pushes:
        copy.wait()


def hand(arrays, cuts):
    anywhere = pl.BlockSpec(memory_space=pl.ANY)
    return pl.pallas_call(
        functools.partial(hand_kernel, cuts),
        out_shape=[jax.ShapeDtypeStruct(a.shape, a.dtype) for a in arrays],
        in_specs=[anywhere] * len(arrays),
        out_specs=[anywhere] * len(arrays),
        scratch_shapes=[pltpu.VMEM(a.shape, a.dtype) for a in arrays]
        + [pltpu.SemaphoreType.DMA((sum(cuts),))] * 2,
        compiler_params=pltpu.CompilerParams(vmem_limit_bytes=60 * 1024 * 1024),
        name="hand",
    )(*arrays)


def local(signal, lengths, w_conv, w_res, w_in, w_qkv, w_out, d_out):
    samples, chans = signal.shape[1:]
    toks, width = d_out.shape[1:]
    flat, grad = signal.reshape(samples, chans), d_out.reshape(toks, width)
    heads = w_out.shape[0] // (width // HEADS)
    gates, edge, hsum, pool, ctx, cols, lens, w_convt, w_qkvt = front(
        lengths, flat, w_qkv, w_conv, w_out, w_res, grad, 0
    )
    weights = (w_convt, w_res, w_in, w_qkv, w_qkvt, w_out)
    results = back(
        lengths, lens, flat, edge, gates, hsum, pool, ctx, cols, weights, grad, heads, 1
    )
    out, d_sig, *grads = hand(results, (1, 3, 1, 1, 1, 1, 1))
    return (out[None], d_sig[None], *grads)


def solution(mesh):
    in_specs = (
        P("stream", "tm", None),
        P("stream"),
        P(),
        P(),
        P(),
        P(None, "stream"),
        P("stream", None),
        P("stream", "tm", None),
    )
    out_specs = (
        P("stream", "tm", None),
        P("stream", "tm", None),
        P("stream", None),
        P("stream", None),
        P("stream", None),
        P("tm", "stream"),
        P("stream", "tm"),
    )
    return jax.shard_map(local, mesh=mesh, in_specs=in_specs, out_specs=out_specs, check_vma=False)
```

```python
import functools
import math

import jax
import jax.numpy as jnp
from jax import lax
from jax.experimental import pallas as pl
from jax.experimental.pallas import tpu as pltpu
from jax.sharding import PartitionSpec as P

HEADS = 16
POOL = 256
DILATION_STEP = 512
EPS = 1e-05
BF16 = jnp.bfloat16
F32 = jnp.float32
MESH = pl.DeviceIdType.MESH
VMEM_SPEC = pl.BlockSpec(memory_space=pltpu.VMEM)


def device_of(tm, stream):
    return {"tm": tm, "stream": stream}


def front_kernel(
    steps, group, len_ref, sig_hbm, wqkv_hbm, w_ref, wout_ref, wres_ref, wgrad_ref,
    a_hbm, edge_hbm, hsum_ref, pool_ref, ctx_ref, cols_ref, lens_ref, wt_ref, wqkvt_ref,
    sig, a_buf, grads, grads_f, wqkv, gate_w, ctx_mine, cols_mine, sums, sem_in, sem_out, send_tm, recv_tm,
    send_st, recv_st, send_pool, recv_pool, send_near, recv_near, keep,
):
    tms, parts = lax.axis_size("tm"), lax.axis_size("stream")
    tm, st = lax.axis_index("tm"), lax.axis_index("stream")
    chips = parts // 2
    core, chip = lax.rem(st, 2), st // 2
    mine = tm * chips + chip
    tile = DILATION_STEP
    samples = steps * tile
    chans = w_ref.shape[1] // 2
    toks = samples // POOL
    rounds = steps // group

    def peer_of(flat):
        return device_of(flat // chips, lax.rem(flat, chips) * 2 + core)

    barrier = pltpu.get_barrier_semaphore()

    def greet(device):
        pl.semaphore_signal(barrier, inc=1, device_id=device, device_id_type=MESH)

    others = tms * chips
    lax.fori_loop(1, others, lambda d, c: (greet(peer_of(lax.rem(mine + d, others))), c)[1], 0)
    for d in range(chips):
        greet(device_of(tm, lax.rem(chip + d, chips) * 2 + 1 - core))

    def load(i):
        return pltpu.make_async_copy(
            sig_hbm.at[pl.ds(i * tile, tile)], sig.at[pl.ds((i + 1) * tile, tile)], sem_in.at[i]
        )

    def save(i):
        return pltpu.make_async_copy(
            a_buf.at[pl.ds(i * tile, tile)], a_hbm.at[pl.ds(i * tile, tile)], sem_out.at[i]
        )

    for i in reversed(range(steps)):
        load(i).start()
    fetch = pltpu.make_async_copy(wqkv_hbm, wqkv, keep.at[4])
    fetch.start()
    gate_w[...] = w_ref[:, chans:] * jnp.asarray(0.5, BF16)

    halo = pltpu.make_async_remote_copy(
        src_ref=sig_hbm.at[pl.ds(samples - tile, tile)],
        dst_ref=sig.at[pl.ds(0, tile)],
        send_sem=send_tm.at[2, 0],
        recv_sem=recv_tm.at[2, 0],
        device_id={"tm": lax.rem(tm + 1, tms)},
        device_id_type=MESH,
    )

    def to_stream(j, d, src, dst):
        return pltpu.make_async_remote_copy(
            src_ref=src,
            dst_ref=dst,
            send_sem=send_st.at[j, d - 1],
            recv_sem=recv_st.at[j, d - 1],
            device_id={"stream": lax.rem(st + d, parts)},
            device_id_type=MESH,
        )

    grad_copies = [
        copy
        for d in range(1, parts)
        for copy in (
            to_stream(0, d, wgrad_ref, grads.at[st]),
            to_stream(1, d, lens_ref.at[st], lens_ref.at[st]),
        )
    ]

    def to_tm(j, d, src, dst, device):
        return pltpu.make_async_remote_copy(
            src_ref=src,
            dst_ref=dst,
            send_sem=send_tm.at[j, d - 1],
            recv_sem=recv_tm.at[j, d - 1],
            device_id=device,
            device_id_type=MESH,
        )

    width = grads.shape[2]
    columns = width // tms

    pairs = tms // 2
    across = {"tm": tm + 1 - 2 * lax.rem(tm, 2)}
    ctx_copies = [
        to_tm(0, d, ctx_mine, ctx_ref.at[tm], {"tm": lax.rem(tm + 2 * d, tms)})
        for d in range(1, pairs)
    ]
    ctx_passes = []
    for d in range(pairs):
        block = ctx_ref.at[lax.rem(tm - 2 * d + tms, tms)]
        ctx_passes.append(to_tm(0, pairs + d, block if d else ctx_mine, block, across))
    cols_copies = [
        to_tm(
            1, d, cols_mine.at[lax.rem(tm + d, tms)], cols_ref.at[st, tm],
            {"tm": lax.rem(tm + d, tms)},
        )
        for d in range(1, tms)
    ]
    cols_shares = [to_stream(2, d, cols_ref.at[st], cols_ref.at[st]) for d in range(1, parts)]
    own_grad = pltpu.make_async_copy(wgrad_ref, grads.at[st], keep.at[0])
    own_ctx = pltpu.make_async_copy(ctx_mine, ctx_ref.at[tm], keep.at[1])
    own_cols = pltpu.make_async_copy(cols_mine.at[tm], cols_ref.at[st, tm], keep.at[2])
    edge = pltpu.make_async_copy(sig.at[pl.ds(0, tile)], edge_hbm, keep.at[3])

    for k in range(tms):
        cols_mine[k] = wgrad_ref[:, k * columns : (k + 1) * columns]
    lens_ref[st] = jnp.full(lens_ref.shape[1:], len_ref[0], jnp.int32)
    length = len_ref[0]

    def chunk(token):
        base = token * POOL
        past = sig[pl.ds(base, POOL), :]
        cur = sig[pl.ds(base + tile, POOL), :]
        mixed_f = jnp.dot(past, w_ref[:chans, :chans], preferred_element_type=F32)
        mixed_f += jnp.dot(cur, w_ref[chans:, :chans], preferred_element_type=F32)
        mixed_g = jnp.dot(past, gate_w[:chans], preferred_element_type=F32)
        mixed_g += jnp.dot(cur, gate_w[chans:], preferred_element_type=F32)
        row = lax.broadcasted_iota(jnp.int32, (POOL, 128), 0) + (tm * samples + base)
        half = jnp.where(row < length, 0.5, 0.0)
        half = jnp.concatenate([half] * (chans // 128), axis=1)
        t = jnp.tanh(mixed_f)
        s = half * jnp.tanh(mixed_g) + half
        h = t * s
        a_buf[pl.ds(base, POOL), :chans] = (s - t * h).astype(BF16)
        a_buf[pl.ds(base, POOL), chans:] = (h - h * s).astype(BF16)
        hs = jnp.sum(h, axis=0, keepdims=True)
        ss = jnp.sum(cur.astype(F32) * half, axis=0, keepdims=True) * 2.0
        return hs, ss

    def body(it, carry):
        r = rounds - 1 - it
        per_tile = tile // POOL
        rows = [None] * (group * per_tile)
        for k in reversed(range(group)):
            i = r * group + k
            if k > 0:
                load(i - 1).wait()
            else:

                @pl.when(r > 0)
                def _():
                    load(i - 1).wait()

                @pl.when((r == 0) & (tm > 0))
                def _():
                    halo.wait_recv()

                @pl.when((r == 0) & (tm == 0))
                def _():
                    sig[pl.ds(0, tile), :] = jnp.zeros((tile, chans), BF16)

            for j in range(per_tile):
                rows[k * per_tile + j] = chunk(i * per_tile + j)
            save(i).start()
        block = pl.ds(pl.multiple_of(r * group * per_tile, 8), group * per_tile)
        hsum_ref[block, :] = jnp.concatenate([a for a, _ in rows], axis=0)
        sums[block, :] = jnp.concatenate([b for _, b in rows], axis=0)

        @pl.when(it == 1)
        def _():
            own_grad.wait()
            for copy in grad_copies:
                copy.wait()
            for p in range(parts):
                grads_f[p * toks : (p + 1) * toks, :] = grads[p].astype(F32)
            d_ctx = lax.dot_general(
                grads_f[...].astype(BF16),
                wout_ref[...],
                (((1,), (1,)), ((), ())),
                preferred_element_type=F32,
            )
            for p in range(parts):
                ctx_mine[p] = d_ctx[p * toks : (p + 1) * toks, :].astype(BF16)
            own_ctx.start()
            for copy in ctx_copies:
                copy.start()
            ctx_passes[0].start()
            own_cols.wait()
            for copy in cols_copies:
                copy.wait()
            for copy in cols_shares:
                copy.start()

        return carry

    pl.semaphore_wait(barrier, others - 1 + chips)

    @pl.when(tm < tms - 1)
    def _():
        halo.start()

    own_grad.start()
    own_cols.start()
    for copy in grad_copies + cols_copies:
        copy.start()
    load(steps - 1).wait()
    lax.fori_loop(0, rounds, body, 0)
    edge.start()

    total = hsum_ref[...]
    high = total.astype(BF16)
    low = (total - high.astype(F32)).astype(BF16)
    resid = jnp.dot(high, wres_ref[...], preferred_element_type=F32)
    resid += jnp.dot(low, wres_ref[...], preferred_element_type=F32)
    pool_ref[st, tm] = ((sums[...] + resid) / POOL).astype(BF16)

    def spread(d):
        return pltpu.make_async_remote_copy(
            src_ref=pool_ref.at[st, tm],
            dst_ref=pool_ref.at[st, tm],
            send_sem=send_pool.at[d],
            recv_sem=recv_pool.at[d],
            device_id=peer_of(lax.rem(mine + d, others)),
            device_id_type=MESH,
        )

    def relay(d):
        flat = lax.rem(mine - d + others, others)
        block = pool_ref.at[lax.rem(flat, chips) * 2 + core, flat // chips]
        return pltpu.make_async_remote_copy(
            src_ref=block,
            dst_ref=block,
            send_sem=send_near.at[d],
            recv_sem=recv_near.at[d],
            device_id={"stream": chip * 2 + 1 - core},
            device_id_type=MESH,
        )

    def launch(d, c):
        spread(d).start()
        return c

    def forward(d, c):
        spread(d).wait_recv()
        relay(d).start()
        return c

    def settle(d, c):
        spread(d).wait_send()
        return c

    def close(d, c):
        relay(d).wait()
        return c

    lax.fori_loop(1, others, launch, 0)
    relay(0).start()
    wt_ref[...] = w_ref[...].T
    fetch.wait()
    wqkvt_ref[...] = wqkv[...].T
    for copy, onward in zip(ctx_copies, ctx_passes[1:]):
        copy.wait_recv()
        onward.start()
    lax.fori_loop(1, others, forward, 0)
    for copy in ctx_copies:
        copy.wait_send()
    for copy in ctx_passes + cols_shares:
        copy.wait()
    own_ctx.wait()
    edge.wait()
    for i in range(steps):
        save(i).wait()

    @pl.when(tm < tms - 1)
    def _():
        halo.wait_send()

    lax.fori_loop(1, others, settle, 0)
    lax.fori_loop(0, others, close, 0)


def front(lengths, signal, w_qkv, w_conv, w_out, w_res, d_out, collective):
    samples, chans = signal.shape
    toks, width = d_out.shape
    tms, parts = lax.axis_size("tm"), lax.axis_size("stream")
    steps = samples // DILATION_STEP
    group = 4
    inner = w_out.shape[0]
    others = tms * parts // 2
    columns = width // tms
    anywhere = pl.BlockSpec(memory_space=pl.ANY)
    dma = pltpu.SemaphoreType.DMA
    return pl.pallas_call(
        functools.partial(front_kernel, steps, group),
        out_shape=[
            jax.ShapeDtypeStruct((samples, 2 * chans), BF16),
            jax.ShapeDtypeStruct((DILATION_STEP, chans), BF16),
            jax.ShapeDtypeStruct((toks, chans), F32),
            jax.ShapeDtypeStruct((parts, tms, toks, chans), BF16),
            jax.ShapeDtypeStruct((tms, parts, toks, inner), BF16),
            jax.ShapeDtypeStruct((parts, tms, toks, columns), BF16),
            jax.ShapeDtypeStruct((parts, 8, 128), jnp.int32),
            jax.ShapeDtypeStruct(w_conv.shape[::-1], BF16),
            jax.ShapeDtypeStruct(w_qkv.shape[::-1], BF16),
        ],
        in_specs=[pl.BlockSpec(memory_space=pltpu.SMEM), anywhere, anywhere] + [VMEM_SPEC] * 4,
        out_specs=[anywhere, anywhere] + [VMEM_SPEC] * 7,
        scratch_shapes=[
            pltpu.VMEM((samples + DILATION_STEP, chans), BF16),
            pltpu.VMEM((samples, 2 * chans), BF16),
            pltpu.VMEM((parts, toks, width), BF16),
            pltpu.VMEM((parts * toks, width), F32),
            pltpu.VMEM(w_qkv.shape, BF16),
            pltpu.VMEM((2 * chans, chans), BF16),
            pltpu.VMEM((parts, toks, inner), BF16),
            pltpu.VMEM((tms, toks, columns), BF16),
            pltpu.VMEM((toks, chans), F32),
            dma((steps,)),
            dma((steps,)),
            dma((3, tms - 1)),
            dma((3, tms - 1)),
            dma((3, parts - 1)),
            dma((3, parts - 1)),
            dma((others,)),
            dma((others,)),
            dma((others,)),
            dma((others,)),
            dma((5,)),
        ],
        compiler_params=pltpu.CompilerParams(collective_id=collective, has_side_effects=True),
        name="front",
    )(lengths, signal, w_qkv, w_conv, w_out, w_res, d_out)


NT = (((1,), (1,)), ((), ()))
TN = (((0,), (0,)), ((), ()))


def fdot(a, b, dims=(((1,), (0,)), ((), ()))):
    return lax.dot_general(a, b, dims, preferred_element_type=F32)


def attend(heads, size, allowed, proj, dctx, ctx, dproj):
    scale = 1.0 / math.sqrt(size)
    span = range(heads)

    def part(h, j):
        base = (3 * h + j) * size
        return proj[:, base : base + size]

    inner = [slice(h * size, (h + 1) * size) for h in span]
    scores = [fdot(part(h, 0), part(h, 1), NT) * scale for h in span]
    d_prob = [fdot(dctx[:, inner[h]], part(h, 2), NT) for h in span]
    scores = [jnp.where(allowed, a, -1e30) for a in scores]
    weights = [jnp.exp(a - jnp.max(a, axis=-1, keepdims=True)) for a in scores]
    prob = [a * (1.0 / jnp.sum(a, axis=-1, keepdims=True)) for a in weights]
    prob16 = [a.astype(BF16) for a in prob]
    d_score = [
        (p * (d - jnp.sum(d * p, axis=-1, keepdims=True))).astype(BF16)
        for p, d in zip(prob, d_prob)
    ]
    for h in span:
        base = 3 * h * size
        ctx[:, inner[h]] = fdot(prob16[h], part(h, 2))
        d_query = scale * fdot(d_score[h], part(h, 1))
        d_key = scale * fdot(d_score[h], part(h, 0), TN)
        d_value = fdot(prob16[h], dctx[:, inner[h]], TN)
        dproj[:, base : base + size] = d_query.astype(BF16)
        dproj[:, base + size : base + 2 * size] = d_key.astype(BF16)
        dproj[:, base + 2 * size : base + 3 * size] = d_value.astype(BF16)


def back_kernel(
    steps, heads, len_ref, lens_ref, sig_hbm, edge_hbm, a_hbm, hsum_ref, pool_ref, ctx_hbm, cols_hbm,
    wt_hbm, wres_ref, win_ref, wqkv_hbm, wqkvt_hbm, wout_hbm, grad_ref,
    out_ref, dsig_hbm, gconv_ref, gres_ref, gin_ref, gqkv_ref, gout_ref,
    sig, a_buf, dsig, first, arrive, pool_f, pool_b, dctx_f, dctx_b, cols_f, cols_b, tok_v, norm,
    proj, ctx_v, dproj, dg, gin_acc, cols_acc, own_send, own_land, out_send, out_land, cols_mine,
    cols_land, in_parts, in_near, in_sum, in_far, conv_acc, conv_parts, conv_near, conv_sum,
    conv_far, conv_f, conv_rows, conv_rland, conv_own, conv_land, res_acc, res_parts, res_near,
    res_sum, res_far, res_f, res_rows, res_rland, res_own, res_land, dh8, dr8, turned, rate,
    ctx_in, cols_in, wt_ref, wqkv_ref, wqkvt_ref, wout_ref, sem_w,
    sem_in, sem_a, sem_out, send, recv,
):
    tms, parts = lax.axis_size("tm"), lax.axis_size("stream")
    tm, st = lax.axis_index("tm"), lax.axis_index("stream")
    chips = parts // 2
    core, chip = lax.rem(st, 2), st // 2
    tile = DILATION_STEP
    samples = steps * tile
    chans = wt_ref.shape[1] // 2
    toks, width = grad_ref.shape
    total = tms * toks
    inner = wout_ref.shape[0]
    size = inner // heads
    columns = width // tms
    in_rows = chans // parts

    barrier = pltpu.get_barrier_semaphore()
    for d in range(1, parts):
        pl.semaphore_signal(
            barrier, inc=1, device_id={"stream": lax.rem(st + d, parts)}, device_id_type=MESH
        )
    for d in range(1, tms):
        pl.semaphore_signal(
            barrier, inc=1, device_id={"tm": lax.rem(tm + d, tms)}, device_id_type=MESH
        )

    names = ("wqkv", "ctx", "cols", "wqkvt", "wout", "wt")
    sources = (wqkv_hbm, ctx_hbm, cols_hbm, wqkvt_hbm, wout_hbm, wt_hbm)
    targets = (wqkv_ref, ctx_in, cols_in, wqkvt_ref, wout_ref, wt_ref)
    pending = {
        name: pltpu.make_async_copy(src, dst, sem_w.at[k])
        for k, (name, src, dst) in enumerate(zip(names, sources, targets))
    }
    for copy in pending.values():
        copy.start()

    def need(*wanted):
        for name in wanted:
            if name in pending:
                pending.pop(name).wait()

    loads = [pltpu.make_async_copy(edge_hbm, sig.at[pl.ds(0, tile)], sem_in.at[0])]
    loads.append(pltpu.make_async_copy(sig_hbm, sig.at[pl.ds(tile, samples)], sem_in.at[1]))
    loads.append(pltpu.make_async_copy(a_hbm, a_buf, sem_a.at[0]))
    for copy in loads:
        copy.start()

    count = iter(range(send.shape[0]))

    def remote(src, dst, device):
        j = next(count)
        return pltpu.make_async_remote_copy(
            src_ref=src,
            dst_ref=dst,
            send_sem=send.at[j],
            recv_sem=recv.at[j],
            device_id=device,
            device_id_type=MESH,
        )

    def to_stream(d):
        return {"stream": lax.rem(st + d, parts)}

    def to_tm(d):
        return {"tm": lax.rem(tm + d, tms)}

    def to_chip(d):
        return {"stream": lax.rem(chip + d, chips) * 2 + core}

    near = {"stream": chip * 2 + 1 - core}

    def begin(copies):
        for copy in copies:
            copy.start()

    def finish(copies):
        for copy in copies:
            copy.wait()

    row = lax.broadcasted_iota(jnp.int32, (total, total), 0)
    col = lax.broadcasted_iota(jnp.int32, (total, total), 1)
    gout_ref[...] = jnp.zeros_like(gout_ref)
    gqkv_ref[...] = jnp.zeros_like(gqkv_ref)
    gin_acc[...] = jnp.zeros_like(gin_acc)
    cols_acc[...] = jnp.zeros_like(cols_acc)
    batch = pool_b.shape[0] // total

    def lead(b):
        for s in range(batch):
            for k in range(tms):
                rows = slice(s * total + k * toks, s * total + (k + 1) * toks)
                pool_f[rows, :] = pool_ref[b * batch + s, k].astype(F32)
        pool_b[...] = pool_f[...].astype(BF16)
        tok_v[...] = fdot(pool_b[...], win_ref[...]).astype(BF16).astype(F32)

        def scaled(s, c):
            rows = pl.ds(pl.multiple_of(s * total, total), total)
            tok = tok_v[rows, :]
            r = lax.rsqrt(jnp.mean(tok * tok, axis=-1, keepdims=True) + EPS)
            norm[rows, :] = (tok * r).astype(BF16)
            rate[rows, :] = jnp.broadcast_to(r, (total, 128))
            return c

        lax.fori_loop(0, batch, scaled, 0)
        need("wqkv", "ctx", "cols")
        proj[...] = fdot(norm[...], wqkv_ref[...]).astype(BF16)
        for s in range(batch):
            for k in range(tms):
                rows = slice(s * total + k * toks, s * total + (k + 1) * toks)
                dctx_f[rows, :] = ctx_in[k, b * batch + s].astype(F32)
                cols_f[rows, :] = cols_in[b * batch + s, k].astype(F32)
        dctx_b[...] = dctx_f[...].astype(BF16)
        cols_b[...] = cols_f[...].astype(BF16)

        def look(s, c):
            rows = pl.ds(pl.multiple_of(s * total, total), total)
            limit = lens_ref[b * batch + s, 0:1, 0:1]
            allowed = (col <= row) & (col * POOL < limit)
            attend(
                heads, size, allowed, proj.at[rows], dctx_b.at[rows], ctx_v.at[rows], dproj.at[rows]
            )
            return c

        lax.fori_loop(0, batch, look, 0)
        need("wqkvt")
        dg[...] = fdot(dproj[...], wqkvt_ref[...])

        def through(s, c):
            rows = pl.ds(pl.multiple_of(s * total, total), total)
            own = pl.ds(pl.multiple_of(s * total + tm * toks, 8), toks)
            d_normed, tok = dg[rows, :], tok_v[rows, :]
            r = rate[rows, 0:1]
            along = jnp.sum(d_normed * tok, axis=-1, keepdims=True)
            dg[rows, :] = r * d_normed - tok * (r * r * r * along / width)
            own_send[b * batch + s] = dg[own, :].astype(BF16)
            return c

        lax.fori_loop(0, batch, through, 0)

    def follow(b):
        need("wout")
        for s in range(batch):
            own = pl.ds(pl.multiple_of(s * total + tm * toks, 8), toks)
            value = fdot(ctx_v[own, :].astype(BF16), wout_ref[...])
            out_send[b * batch + s] = value.astype(BF16)
        gin_acc[...] += fdot(pool_b[...], dg[...].astype(BF16), TN)
        cols_acc[...] += fdot(pool_b[...], cols_b[...], TN)

    def weights(b):
        gout_ref[...] += fdot(ctx_v[...].astype(BF16), cols_b[...], TN)
        if columns % 128 == 0:
            own = norm[:, pl.ds(pl.multiple_of(tm * columns, columns), columns)]
            gqkv_ref[...] += fdot(own, dproj[...], TN)
        else:
            for k in range(tms):

                @pl.when(tm == k)
                def _():
                    own = norm[:, k * columns : (k + 1) * columns]
                    gqkv_ref[...] += fdot(own, dproj[...], TN)

    batches = parts // batch

    def whole_batch(b, c):
        lead(b)
        follow(b)
        weights(b)
        return c

    if batches > 1:
        need(*names)
        lax.fori_loop(0, batches - 1, whole_batch, 0)
    lead(batches - 1)

    own_copies = [
        remote(own_send.at[lax.rem(st + d, parts)], own_land.at[d - 1], to_stream(d))
        for d in range(1, parts)
    ]
    out_copies = [
        remote(out_send.at[lax.rem(st + d, parts)], out_land.at[d - 1], to_stream(d))
        for d in range(1, parts)
    ]
    cols_copies = [remote(cols_mine, cols_land.at[tm], to_tm(d)) for d in range(1, tms)]
    back = remote(first, arrive, {"tm": lax.rem(tm + tms - 1, tms)})

    def reduce_near(blocks, land):
        return [remote(blocks.at[1 - core], land, near)]

    def reduce_far(sums, land):
        return [
            remote(sums.at[lax.rem(chip + d, chips)], land.at[d - 1], to_chip(d))
            for d in range(1, chips)
        ]

    in_one = reduce_near(in_parts, in_near)
    in_two = reduce_far(in_sum, in_far)
    conv_one = reduce_near(conv_parts, conv_near) + reduce_near(res_parts, res_near)
    conv_two = reduce_far(conv_sum, conv_far) + reduce_far(res_sum, res_far)
    conv_three = [
        copy
        for d in range(1, tms)
        for copy in (
            remote(conv_rows.at[lax.rem(tm + d, tms)], conv_rland.at[d - 1], to_tm(d)),
            remote(res_rows.at[lax.rem(tm + d, tms)], res_rland.at[d - 1], to_tm(d)),
        )
    ]
    conv_four = [
        copy
        for d in range(1, tms)
        for copy in (
            remote(conv_own, conv_land.at[tm], to_tm(d)),
            remote(res_own, res_land.at[tm], to_tm(d)),
        )
    ]

    def split(acc, blocks):
        rows = blocks.shape[2]
        for c in range(2):
            for q in range(chips):
                base = (q * 2 + c) * rows
                blocks[c, q] = acc[base : base + rows, :].astype(BF16)

    def add_near(blocks, land, sums):
        for q in range(chips):
            sums[q] = (blocks[core, q].astype(F32) + land[q].astype(F32)).astype(BF16)

    def add_far(sums, land):
        value = sums[chip].astype(F32)
        for d in range(1, chips):
            value += land[d - 1].astype(F32)
        return value

    def cut(value, full, rows):
        full[...] = value
        n = rows.shape[1]
        for k in range(tms):
            rows[k] = full[k * n : (k + 1) * n, :].astype(BF16)

    def add_rows(rows, land, own, gathered):
        value = rows[tm].astype(F32)
        for d in range(1, tms):
            value += land[d - 1].astype(F32)
        own[...] = value.astype(BF16)
        gathered[tm] = value.astype(BF16)

    pl.semaphore_wait(barrier, parts - 1 + tms - 1)
    begin(own_copies)
    follow(batches - 1)
    split(gin_acc, in_parts)
    cols_mine[...] = cols_acc[pl.ds(pl.multiple_of(st * in_rows, 8), in_rows), :].astype(BF16)
    cols_land[tm] = cols_mine[...]
    begin(in_one)
    begin(out_copies)
    begin(cols_copies)
    own_tok = fdot(pool_ref[st, tm], win_ref[...]).astype(BF16).astype(F32)

    finish(own_copies)
    d_tok = own_send[st].astype(F32) + grad_ref[...].astype(F32)
    for d in range(1, parts):
        d_tok += own_land[d - 1].astype(F32)
    d_pooled = fdot(d_tok.astype(BF16), win_ref[...], NT)
    d_res = (d_pooled / POOL).astype(BF16)
    d_hidden = fdot(d_res, wres_ref[...], NT)
    d_resf = d_res.astype(F32)
    for t in range(toks):
        dh8[t] = jnp.broadcast_to(d_hidden[t : t + 1, :], (8, chans))
        dr8[t] = jnp.broadcast_to(d_resf[t : t + 1, :], (8, chans))
    high = hsum_ref[...].astype(BF16)
    low = (hsum_ref[...] - high.astype(F32)).astype(BF16)
    res_acc[...] = fdot(high, d_res, TN) + fdot(low, d_res, TN)
    split(res_acc, res_parts)

    finish(in_one)
    add_near(in_parts, in_near, in_sum)
    begin(in_two)
    finish(loads)
    need("wt")

    per_tile = tile // POOL

    def later_of(i):
        return fdot(a_buf[pl.ds(i * tile, tile), :], wt_ref[:, :chans]).astype(BF16)

    conv_acc[...] = jnp.zeros_like(conv_acc)
    turned[:chans, :] = sig[pl.ds(0, tile), :].T

    def weigh(i, carry):
        rows = pl.ds(i * tile, tile)
        for j in range(per_tile):
            token = i * per_tile + j
            base = pl.ds(token * POOL, POOL)
            gate = dh8[token]
            for c in range(2):
                lanes = slice(c * chans, (c + 1) * chans)
                a = a_buf[base, lanes].astype(F32).reshape(POOL // 8, 8, chans)
                a_buf[base, lanes] = (a * gate[None]).reshape(POOL, chans).astype(BF16)
        dm = a_buf[rows, :]
        turned[chans:, :] = sig[pl.ds((i + 1) * tile, tile), :].T
        conv_acc[...] += fdot(turned[...], dm)
        turned[:chans, :] = turned[chans:, :]

        @pl.when(i == 0)
        def _():
            first[...] = later_of(0)

            @pl.when(tm > 0)
            def _():
                back.start()

        return carry

    lax.fori_loop(0, steps, weigh, 0)

    split(conv_acc, conv_parts)
    begin(conv_one)
    weights(batches - 1)

    length = len_ref[0]

    def emit(i, later):
        rows = pl.ds(i * tile, tile)
        here = fdot(a_buf[rows, :], wt_ref[:, chans:])
        for j in range(per_tile):
            token = i * per_tile + j
            index = lax.broadcasted_iota(jnp.int32, (POOL, 128), 0) + (tm * samples + token * POOL)
            valid = jnp.where(index < length, 1.0, 0.0)
            valid = jnp.concatenate([valid] * (chans // 128), axis=1)
            own = dr8[token][None] * valid.reshape(POOL // 8, 8, chans)
            part = slice(j * POOL, (j + 1) * POOL)
            value = own.reshape(POOL, chans) + here[part] + later[part].astype(F32)
            dsig[pl.ds(token * POOL, POOL), :] = value.astype(BF16)
        pltpu.make_async_copy(dsig.at[rows], dsig_hbm.at[rows], sem_out.at[i]).start()

    def emit_step(i, carry):
        emit(i, later_of(i + 1))
        return carry

    cuts = [0, steps // 12, steps // 3, steps - 1]
    lax.fori_loop(cuts[0], cuts[1], emit_step, 0)
    finish(conv_one)
    add_near(conv_parts, conv_near, conv_sum)
    add_near(res_parts, res_near, res_sum)
    begin(conv_two)
    lax.fori_loop(cuts[1], cuts[2], emit_step, 0)
    finish(in_two)
    finish(conv_two)
    cut(add_far(conv_sum, conv_far), conv_f, conv_rows)
    cut(add_far(res_sum, res_far), res_f, res_rows)
    begin(conv_three)
    lax.fori_loop(cuts[2], cuts[3], emit_step, 0)

    @pl.when(tm < tms - 1)
    def _():
        back.wait_recv()

    @pl.when(tm == tms - 1)
    def _():
        arrive[...] = jnp.zeros_like(arrive)

    emit(steps - 1, arrive[...])
    finish(out_copies)
    value = own_tok + out_send[st].astype(F32)
    for d in range(1, parts):
        value += out_land[d - 1].astype(F32)
    out_ref[...] = value.astype(BF16)
    finish(cols_copies)
    total_in = add_far(in_sum, in_far)
    for k in range(tms):
        lanes = slice(k * columns, (k + 1) * columns)
        gin_ref[:, lanes] = total_in[:, lanes] + cols_land[k].astype(F32)

    finish(conv_three)
    add_rows(conv_rows, conv_rland, conv_own, conv_land)
    add_rows(res_rows, res_rland, res_own, res_land)
    begin(conv_four)

    @pl.when(tm > 0)
    def _():
        back.wait_send()

    for i in range(steps):
        rows = pl.ds(i * tile, tile)
        pltpu.make_async_copy(dsig.at[rows], dsig_hbm.at[rows], sem_out.at[i]).wait()
    finish(conv_four)
    for k in range(tms):
        n = conv_land.shape[1]
        gconv_ref[k * n : (k + 1) * n, :] = conv_land[k].astype(F32)
        n = res_land.shape[1]
        gres_ref[k * n : (k + 1) * n, :] = res_land[k].astype(F32)


def back(lengths, lens, signal, edge, gates, hsum, pool, ctx, cols, weights, d_out, heads, collective):
    w_convt, w_res, w_in, w_qkv, w_qkvt, w_out = weights
    samples, chans = signal.shape
    toks, width = d_out.shape
    tms, parts = lax.axis_size("tm"), lax.axis_size("stream")
    chips = parts // 2
    steps = samples // DILATION_STEP
    total = toks * tms
    rows = total * max(n for n in range(1, parts + 1) if parts % n == 0 and (n == 1 or n * total <= 768))
    inner = w_out.shape[0]
    triple = w_qkv.shape[1]
    columns = width // tms
    joined = 2 * chans
    conv_n, res_n = joined // parts, chans // parts
    anywhere = pl.BlockSpec(memory_space=pl.ANY)
    dma = pltpu.SemaphoreType.DMA

    def vm(*shape, dtype=BF16):
        return pltpu.VMEM(shape, dtype)

    def reduction(size, n, lanes):
        return [
            vm(size, lanes, dtype=F32),
            vm(2, chips, n, lanes),
            vm(chips, n, lanes),
            vm(chips, n, lanes),
            vm(max(chips - 1, 1), n, lanes),
            vm(n, lanes, dtype=F32),
            vm(tms, n // tms, lanes),
            vm(tms - 1, n // tms, lanes),
            vm(n // tms, lanes),
            vm(tms, n // tms, lanes),
        ]

    copies = 2 * (parts - 1) + 5 * (tms - 1) + 1 + 3 + 3 * (chips - 1)
    return pl.pallas_call(
        functools.partial(back_kernel, steps, heads),
        out_shape=[
            jax.ShapeDtypeStruct((toks, width), BF16),
            jax.ShapeDtypeStruct((samples, chans), BF16),
            jax.ShapeDtypeStruct((conv_n, joined), F32),
            jax.ShapeDtypeStruct((res_n, chans), F32),
            jax.ShapeDtypeStruct((res_n, width), F32),
            jax.ShapeDtypeStruct((columns, triple), F32),
            jax.ShapeDtypeStruct((inner, columns), F32),
        ],
        in_specs=[pl.BlockSpec(memory_space=pltpu.SMEM), VMEM_SPEC]
        + [anywhere] * 3
        + [VMEM_SPEC] * 2
        + [anywhere] * 3
        + [VMEM_SPEC] * 2
        + [anywhere] * 3
        + [VMEM_SPEC],
        out_specs=[VMEM_SPEC, anywhere] + [VMEM_SPEC] * 5,
        scratch_shapes=[
            vm(samples + DILATION_STEP, chans),
            vm(samples, joined),
            vm(samples, chans),
            vm(DILATION_STEP, chans),
            vm(DILATION_STEP, chans),
            vm(rows, chans, dtype=F32),
            vm(rows, chans),
            vm(rows, inner, dtype=F32),
            vm(rows, inner),
            vm(rows, columns, dtype=F32),
            vm(rows, columns),
            vm(rows, width, dtype=F32),
            vm(rows, width),
            vm(rows, triple),
            vm(rows, inner, dtype=F32),
            vm(rows, triple),
            vm(rows, width, dtype=F32),
            vm(chans, width, dtype=F32),
            vm(chans, columns, dtype=F32),
            vm(parts, toks, width),
            vm(parts - 1, toks, width),
            vm(parts, toks, width),
            vm(parts - 1, toks, width),
            vm(res_n, columns),
            vm(tms, res_n, columns),
            vm(2, chips, res_n, width),
            vm(chips, res_n, width),
            vm(chips, res_n, width),
            vm(max(chips - 1, 1), res_n, width),
        ]
        + reduction(joined, conv_n, joined)
        + reduction(chans, res_n, chans)
        + [
            vm(toks, 8, chans, dtype=F32),
            vm(toks, 8, chans, dtype=F32),
            vm(joined, DILATION_STEP),
            vm(rows, 128, dtype=F32),
            vm(*ctx.shape),
            vm(*cols.shape),
            vm(*w_convt.shape),
            vm(*w_qkv.shape),
            vm(*w_qkvt.shape),
            vm(*w_out.shape),
            dma((6,)),
            dma((2,)),
            dma((1,)),
            dma((steps,)),
            dma((copies,)),
            dma((copies,)),
        ],
        compiler_params=pltpu.CompilerParams(
            collective_id=collective, has_side_effects=True, vmem_limit_bytes=60 * 1024 * 1024
        ),
        name="back",
    )(lengths, lens, signal, edge, gates, hsum, pool, ctx, cols, *weights, d_out)


def hand_kernel(cuts, *refs):
    n = len(cuts)
    ins, outs, bufs, (sem_in, sem_out) = refs[:n], refs[n : 2 * n], refs[2 * n : 3 * n], refs[3 * n :]
    pulls, pushes = [], []
    for j, pieces in enumerate(cuts):
        rows = ins[j].shape[0] // pieces
        for k in range(pieces):
            part = pl.ds(k * rows, rows)
            at = len(pulls)
            pulls.append(
                pltpu.make_async_copy(ins[j].at[part], bufs[j].at[part], sem_in.at[at])
            )
            pushes.append(
                pltpu.make_async_copy(bufs[j].at[part], outs[j].at[part], sem_out.at[at])
            )
    for copy in pulls:
        copy.start()
    for pull, push in zip(pulls, pushes):
        pull.wait()
        push.start()
    for copy in pushes:
        copy.wait()


def hand(arrays, cuts):
    anywhere = pl.BlockSpec(memory_space=pl.ANY)
    return pl.pallas_call(
        functools.partial(hand_kernel, cuts),
        out_shape=[jax.ShapeDtypeStruct(a.shape, a.dtype) for a in arrays],
        in_specs=[anywhere] * len(arrays),
        out_specs=[anywhere] * len(arrays),
        scratch_shapes=[pltpu.VMEM(a.shape, a.dtype) for a in arrays]
        + [pltpu.SemaphoreType.DMA((sum(cuts),))] * 2,
        compiler_params=pltpu.CompilerParams(vmem_limit_bytes=60 * 1024 * 1024),
        name="hand",
    )(*arrays)


def local(signal, lengths, w_conv, w_res, w_in, w_qkv, w_out, d_out):
    samples, chans = signal.shape[1:]
    toks, width = d_out.shape[1:]
    flat, grad = signal.reshape(samples, chans), d_out.reshape(toks, width)
    heads = w_out.shape[0] // (width // HEADS)
    gates, edge, hsum, pool, ctx, cols, lens, w_convt, w_qkvt = front(
        lengths, flat, w_qkv, w_conv, w_out, w_res, grad, 0
    )
    weights = (w_convt, w_res, w_in, w_qkv, w_qkvt, w_out)
    results = back(
        lengths, lens, flat, edge, gates, hsum, pool, ctx, cols, weights, grad, heads, 1
    )
    out, d_sig, *grads = hand(results, (1, 3, 1, 1, 1, 1, 1))
    return (out[None], d_sig[None], *grads)


def solution(mesh):
    in_specs = (
        P("stream", "tm", None),
        P("stream"),
        P(),
        P(),
        P(),
        P(None, "stream"),
        P("stream", None),
        P("stream", "tm", None),
    )
    out_specs = (
        P("stream", "tm", None),
        P("stream", "tm", None),
        P("stream", None),
        P("stream", None),
        P("stream", None),
        P("tm", "stream"),
        P("stream", "tm"),
    )
    return jax.shard_map(local, mesh=mesh, in_specs=in_specs, out_specs=out_specs, check_vma=False)
```
